256 devices in a mesh: expert: 64 (over z, y, core), etp: 4 (over x).
Axes of the slice: x: 4, y: 4, z: 8, core: 2. Of those that a mesh axis runs over, the one named last changes fastest.
Arguments:
- tokens: bfloat16 [32768, 2560], P(('expert', 'etp')), may hold values from -6 to 6
- hidden_grad: bfloat16 [32768, 4096], P(('expert', 'etp')), may hold values from -6 to 6
- routes: int32 [32768, 1], P(('expert', 'etp')), may hold values from 0 to 63; in each aligned block of 512 rows (0 to 511, 512 to 1023, ...) at most 10 rows name the same one
- exponents: int32 [32768], P(('expert', 'etp')), may hold values from -2 to 2
- gate_weight: bfloat16 [64, 2560, 4096], P('expert', None, 'etp'), may hold values from -0.125 to 0.125
- up_weight: bfloat16 [64, 2560, 4096], P('expert', None, 'etp'), may hold values from -0.125 to 0.125
Outputs:
- input_grad: bfloat16 [32768, 2560], P(('expert', 'etp'))
The draws below stay inside these ranges and needn't reach their ends.
Inputs may be any that keep to these rules, and one draw needn't show every extreme that they name: `routes`: in each aligned block of 512 rows (the tokens of one group of devices along etp) no expert is named by more than 10 rows, and in every draw some expert is named by exactly 10 rows of some block.
All inputs are finite; a program needn't handle non-finite values.
Results may differ from the reference program's by a relative error of at most 0.0095.
Values may be sent and summed in bfloat16 or wider, within the bound.
No kernel may reach another device: no remote copies, remote signals or barrier semaphores. Data moves between devices by JAX's collectives and lax.ppermute only.
A program may use at most 128 MiB of HBM per device.

```python
import math
import jax
import jax.numpy as jnp
import numpy as np
from jax import lax

D = 2560
FF = 4096
TOK_DEV = 128
EXPERTS = 64
TOKENS = 32768
C = 10
N_EXPERT = 64
N_ETP = 4


def touch_ends(drawn, key, smallest, high):
    longest = drawn.shape.index(max(drawn.shape))
    spots = []
    for shift in (0, 1):
        where = [jax.random.randint(jax.random.fold_in(key, axis), (), 0, length) for axis, length in enumerate(drawn.shape)]
        where[longest] = (where[longest] + shift) % drawn.shape[longest]
        spots.append(tuple(where))
    return drawn.at[spots[0]].set(smallest).at[spots[1]].set(high)


def level_of(key, extent, shards, smallest, largest):
    def one(position, shards_of):
        draws = jax.random.uniform(jax.random.fold_in(jax.random.fold_in(key, 6), position), (shards_of,), jnp.float32, smallest / len(shards), largest / len(shards))
        return jnp.repeat(jnp.exp(draws), extent[position] // shards_of).reshape((-1,) + (1,) * (len(extent) - position - 1))

    level = one(*shards[0])
    for cut in shards[1:]:
        level = level * one(*cut)
    return level


def shared_out(rng, own, number, rows, number_of, top, most, slope):
    order = jax.random.permutation(rng, number_of)
    packed, ordinary = load_shares(number_of, rows * top, most, slope, True), load_shares(number_of, rows * top, most, slope, False)
    places = jnp.arange(number_of)

    def named(lengths, turn):
        used = int((lengths > 0).sum())
        fixed = max(1, used // 4)
        passed = fixed + (places - fixed + turn * (used - fixed)) % max(1, number_of - fixed)
        return jnp.zeros((number_of,), jnp.int32).at[order[jnp.where(places < fixed, places, passed)]].set(jnp.asarray(lengths, jnp.int32))

    lengths = jnp.where(number % 4 == 0, named(packed, number // 4), named(ordinary, number - number // 4 - 1))
    mixed = jax.random.permutation(jax.random.fold_in(own, 3), number_of)
    donor, taker = mixed[0:number_of // 2 * 2:2], mixed[1:number_of // 2 * 2:2]
    room = jnp.minimum(lengths[donor] - 1, most - lengths[taker]) // 2
    room = jnp.where((donor == order[0]) | (taker == order[0]) | (lengths[taker] == 0), 0, jnp.maximum(room, 0))
    passed = jax.random.randint(jax.random.fold_in(own, 4), (number_of // 2,), 0, 1 << 20) % (room + 1)
    lengths = lengths.at[donor].add(-passed).at[taker].add(passed)
    items = jnp.searchsorted(jnp.cumsum(lengths), jnp.arange(rows * top), side="right").astype(jnp.int32)
    grid = items.reshape(top, rows).T
    grid = grid[jax.random.permutation(jax.random.fold_in(own, 1), rows)]
    turn = jax.random.randint(jax.random.fold_in(own, 2), (rows, 1), 0, top)
    return jnp.take_along_axis(grid, (jnp.arange(top)[None, :] + turn) % top, axis=1)


def load_shares(count, total, bound, skew, full):
    loads = [(1 << 20) // math.isqrt(standing ** skew) + 1 for standing in range(1, count + 1)]
    largest = bound if full else min(bound, max(-(-total // count), total * loads[0] // sum(loads)))
    least = 1 if total - largest >= count - 1 else 0
    given, spare = [largest] + [least] * (count - 1), total - largest - least * (count - 1)
    while spare > 0:
        free = [i for i in range(1, count) if given[i] < largest] or [i for i in range(1, count) if given[i] < bound]
        whole, budget = sum([loads[i] for i in free]), spare
        for i in free:
            more = min(bound - given[i], max(1, budget * loads[i] // whole), spare)
            given[i] = given[i] + more
            spare = spare - more
    return np.array(given)


def scatter_about(own_key, dims, deviation, bound, shards=(), kind=jnp.bfloat16):
    level = level_of(own_key, dims, shards, -0.22, 0.18) if shards else 1.0
    values = jax.random.normal(own_key, dims, jnp.float32) * deviation * level
    return jnp.minimum(jnp.maximum(values, -bound), bound).astype(kind)


def setup_inputs(seed: int = 0) -> dict:
    splits = jax.random.split(jax.random.key(seed), 7)
    tokens = scatter_about(splits[0], (TOKENS, D), 1.0, 6.0, ((0, 256),))
    hidden_grad = scatter_about(splits[1], (TOKENS, FF), 1.0, 6.0, ((0, 256),))
    routes_keys = jax.random.split(jax.random.fold_in(splits[2], 1), TOKENS // (N_ETP * TOK_DEV))
    routes_turns = jax.random.permutation(jax.random.fold_in(splits[2], 3), TOKENS // (N_ETP * TOK_DEV))
    routes = jax.vmap(lambda own, number: shared_out(jax.random.fold_in(splits[2], 2), own, number, N_ETP * TOK_DEV, EXPERTS, 1, C, 2))(routes_keys, routes_turns).reshape((TOKENS, 1))
    exponents = touch_ends(jax.random.randint(splits[3], (TOKENS,), -2, 3), jax.random.fold_in(splits[3], 1), -2, 2).astype(jnp.int32)
    gate_weight = scatter_about(splits[4], (EXPERTS, D, FF), D ** -0.5, 0.125, ((0, 64), (2, 4)))
    up_weight = scatter_about(splits[5], (EXPERTS, D, FF), D ** -0.5, 0.125, ((0, 64), (2, 4)))
    return dict(tokens=tokens, hidden_grad=hidden_grad, routes=routes, exponents=exponents, gate_weight=gate_weight, up_weight=up_weight)


def reference(tokens, hidden_grad, routes, exponents, gate_weight, up_weight):
    route_flat = routes[:, 0]
    total = route_flat.shape[0]
    positions = jnp.arange(total, dtype=jnp.int32)
    sorted_ids = jnp.argsort(route_flat * total + positions, stable=True).astype(jnp.int32)
    onehot = (route_flat[:, None] == jnp.arange(EXPERTS, dtype=jnp.int32)[None, :]).astype(jnp.int32)
    counts = jnp.sum(onehot, axis=0).astype(jnp.int32)
    starts = (jnp.cumsum(counts) - counts).astype(jnp.int32)
    slot_limit = N_EXPERT * C
    slot_range = jnp.arange(slot_limit, dtype=jnp.int32)
    scales = jnp.exp2(exponents.astype(jnp.float32))
    quarter = FF // N_ETP

    def per_expert(items):
        w_gate, w_up, row_count, first_row = items
        picked = sorted_ids[jnp.clip(first_row + slot_range, 0, total - 1)]
        live_slot = slot_range < row_count
        picked_rows = tokens[picked]
        scaled_grad = hidden_grad[picked].astype(jnp.float32) * scales[picked][:, None]
        gate_pre = jnp.dot(picked_rows, w_gate, preferred_element_type=jnp.float32)
        up_pre = jnp.dot(picked_rows, w_up, preferred_element_type=jnp.float32)
        sigmoid_gate = jax.nn.sigmoid(gate_pre)
        grad_gate = (scaled_grad * up_pre * sigmoid_gate * (1.0 + gate_pre * (1.0 - sigmoid_gate))).astype(jnp.bfloat16)
        grad_up = (scaled_grad * gate_pre * sigmoid_gate).astype(jnp.bfloat16)
        gate_split = grad_gate.astype(jnp.float32).reshape(slot_limit, N_ETP, quarter)
        up_split = grad_up.astype(jnp.float32).reshape(slot_limit, N_ETP, quarter)
        weight_gate = w_gate.astype(jnp.float32).reshape(D, N_ETP, quarter)
        weight_up = w_up.astype(jnp.float32).reshape(D, N_ETP, quarter)
        partial_value = jnp.einsum("mqf,dqf->qmd", gate_split, weight_gate) + jnp.einsum("mqf,dqf->qmd", up_split, weight_up)
        rounded = lax.optimization_barrier(partial_value.astype(jnp.bfloat16))
        summed = jnp.sum(rounded.astype(jnp.float32), axis=0).astype(jnp.bfloat16)
        target = jnp.where(live_slot, picked, total).astype(jnp.int32)
        return summed, target

    outputs, targets = lax.map(per_expert, (gate_weight, up_weight, counts, starts))
    result = jnp.zeros((total + 1, D), jnp.bfloat16).at[targets.reshape(-1)].set(outputs.reshape(-1, D))
    return result[:total]
```

```python
import jax
import jax.numpy as jnp
from jax import lax
from jax.experimental import pallas as pl
from jax.experimental.pallas import tpu as pltpu
from jax.sharding import PartitionSpec as P

BF = jnp.bfloat16
F32 = jnp.float32
VMEM_LIMIT = 48 * 1024 * 1024


def cost(flops, nbytes, trans=0):
    return pl.CostEstimate(flops=flops, bytes_accessed=nbytes, transcendentals=trans)


def params(grid_rank=1):
    return pltpu.CompilerParams(
        dimension_semantics=("arbitrary",) * grid_rank, vmem_limit_bytes=VMEM_LIMIT
    )


def split_columns(array, quarters, scale=None):
    rows, columns = array.shape
    width = columns // 4

    def kernel(q_ref, *refs):
        scale_refs = refs[4:-4]
        for source, target in zip(refs[:4], refs[-4:]):
            if scale_refs:
                target[...] = (source[...].astype(F32) * scale_refs[0][...]).astype(BF)
            else:
                target[...] = source[...]

    def block(r):
        return pl.BlockSpec((rows, width), lambda i, q: (0, q[r]))

    extra = [] if scale is None else [scale]
    return pl.pallas_call(
        kernel,
        grid_spec=pltpu.PrefetchScalarGridSpec(
            num_scalar_prefetch=1,
            grid=(1,),
            in_specs=[block(r) for r in range(4)]
            + [pl.BlockSpec((rows, 1), lambda i, q: (0, 0)) for _ in extra],
            out_specs=[pl.BlockSpec((rows, width), lambda i, q: (0, 0))] * 4,
        ),
        out_shape=[jax.ShapeDtypeStruct((rows, width), BF)] * 4,
        compiler_params=params(),
        cost_estimate=cost(rows * columns, 4 * rows * columns),
        name="split_columns",
    )(quarters, array, array, array, array, *extra)


def join_columns(blocks, quarters):
    rows, width = blocks[0].shape

    def kernel(q_ref, b0, b1, b2, b3, out):
        for r, block in enumerate((b0, b1, b2, b3)):
            start = pl.multiple_of(q_ref[r] * width, 128)
            out[:, pl.ds(start, width)] = block[...]

    return pl.pallas_call(
        kernel,
        grid_spec=pltpu.PrefetchScalarGridSpec(
            num_scalar_prefetch=1,
            grid=(1,),
            in_specs=[pl.BlockSpec((rows, width), lambda i, q: (0, 0))] * 4,
            out_specs=pl.BlockSpec((rows, 4 * width), lambda i, q: (0, 0)),
        ),
        out_shape=jax.ShapeDtypeStruct((rows, 4 * width), BF),
        compiler_params=params(),
        cost_estimate=cost(0, 16 * rows * width),
        name="join_columns",
    )(quarters, *blocks)


def up_three(blocks, gate_weight, up_weight, quarters):
    rows, depth = blocks[0].shape
    hidden = gate_weight.shape[1]
    tile = 256

    def kernel(q_ref, t0, t1, t2, g0, g1, g2, u0, u1, u2, gate, up):
        for out, weights in ((gate, (g0, g1, g2)), (up, (u0, u1, u2))):
            total = jnp.dot(t0[...], weights[0][...], preferred_element_type=F32)
            total += jnp.dot(t1[...], weights[1][...], preferred_element_type=F32)
            total += jnp.dot(t2[...], weights[2][...], preferred_element_type=F32)
            out[...] = total

    def weight(r):
        return pl.BlockSpec((depth, tile), lambda j, q: (q[r], j))

    whole = pl.BlockSpec((rows, depth), lambda j, q: (0, 0))
    out = pl.BlockSpec((rows, tile), lambda j, q: (0, j))
    return pl.pallas_call(
        kernel,
        grid_spec=pltpu.PrefetchScalarGridSpec(
            num_scalar_prefetch=1,
            grid=(hidden // tile,),
            in_specs=[whole] * 3 + [weight(r) for r in range(3)] * 2,
            out_specs=[out, out],
        ),
        out_shape=[jax.ShapeDtypeStruct((rows, hidden), F32)] * 2,
        compiler_params=params(),
        cost_estimate=cost(12 * rows * depth * hidden, 12 * depth * hidden + 8 * rows * hidden),
        name="up_three",
    )(quarters, *blocks, *([gate_weight] * 3), *([up_weight] * 3))


def up_last(block, gate, up, gate_weight, up_weight, quarters):
    rows, depth = block.shape
    hidden = gate_weight.shape[1]
    tile = 256

    def kernel(q_ref, t, g_in, u_in, wg, wu, for_gate, for_up):
        g = g_in[...] + jnp.dot(t[...], wg[...], preferred_element_type=F32)
        u = u_in[...] + jnp.dot(t[...], wu[...], preferred_element_type=F32)
        s = 1.0 / (1.0 + jnp.exp(-g))
        for_gate[...] = u * s * (1.0 + g * (1.0 - s))
        for_up[...] = g * s

    weight = pl.BlockSpec((depth, tile), lambda j, q: (q[3], j))
    tiled = pl.BlockSpec((rows, tile), lambda j, q: (0, j))
    return pl.pallas_call(
        kernel,
        grid_spec=pltpu.PrefetchScalarGridSpec(
            num_scalar_prefetch=1,
            grid=(hidden // tile,),
            in_specs=[pl.BlockSpec((rows, depth), lambda j, q: (0, 0)), tiled, tiled, weight, weight],
            out_specs=[tiled, tiled],
        ),
        out_shape=[jax.ShapeDtypeStruct((rows, hidden), F32)] * 2,
        compiler_params=params(),
        cost_estimate=cost(
            4 * rows * depth * hidden, 4 * depth * hidden + 16 * rows * hidden, rows * hidden
        ),
        name="up_last",
    )(quarters, block, gate, up, gate_weight, up_weight)


CONTRACT_LAST = (((1,), (1,)), ((), ()))


def down_first(scaled, for_gate, for_up, gate_weight, up_weight, quarters):
    rows, hidden = scaled.shape
    depth = gate_weight.shape[0] // 4
    tile = 160

    def kernel(q_ref, h, a, b, wg, wu, gg_out, gu_out, out):
        scaled_rows = h[...].astype(F32)
        gg = (scaled_rows * a[...]).astype(BF)
        gu = (scaled_rows * b[...]).astype(BF)
        gg_out[...] = gg
        gu_out[...] = gu
        total = lax.dot_general(gg, wg[...], CONTRACT_LAST, preferred_element_type=F32)
        total += lax.dot_general(gu, wu[...], CONTRACT_LAST, preferred_element_type=F32)
        out[...] = total.astype(BF)

    weight = pl.BlockSpec((depth, hidden), lambda i, q: (q[0], 0))
    tiled = pl.BlockSpec((tile, hidden), lambda i, q: (i, 0))
    return pl.pallas_call(
        kernel,
        grid_spec=pltpu.PrefetchScalarGridSpec(
            num_scalar_prefetch=1,
            grid=(rows // tile,),
            in_specs=[tiled, tiled, tiled, weight, weight],
            out_specs=[tiled, tiled, pl.BlockSpec((tile, depth), lambda i, q: (i, 0))],
        ),
        out_shape=[jax.ShapeDtypeStruct((rows, hidden), BF)] * 2
        + [jax.ShapeDtypeStruct((rows, depth), BF)],
        compiler_params=params(),
        cost_estimate=cost(4 * rows * depth * hidden, 4 * depth * hidden + 14 * rows * hidden),
        name="down_first",
    )(quarters, scaled, for_gate, for_up, gate_weight, up_weight)


def down_more(grad_gate, grad_up, gate_weight, up_weight, quarters, count):
    rows, hidden = grad_gate.shape
    depth = gate_weight.shape[0] // 4
    tile = 160

    def kernel(q_ref, gg, gu, *refs):
        for r in range(count):
            wg, wu, out = refs[r], refs[count + r], refs[2 * count + r]
            total = lax.dot_general(gg[...], wg[...], CONTRACT_LAST, preferred_element_type=F32)
            total += lax.dot_general(gu[...], wu[...], CONTRACT_LAST, preferred_element_type=F32)
            out[...] = total.astype(BF)

    def weight(r):
        return pl.BlockSpec((depth, hidden), lambda i, q: (q[r], 0))

    tiled = pl.BlockSpec((tile, hidden), lambda i, q: (i, 0))
    return pl.pallas_call(
        kernel,
        grid_spec=pltpu.PrefetchScalarGridSpec(
            num_scalar_prefetch=1,
            grid=(rows // tile,),
            in_specs=[tiled, tiled] + [weight(r) for r in range(count)] * 2,
            out_specs=[pl.BlockSpec((tile, depth), lambda i, q: (i, 0))] * count,
        ),
        out_shape=[jax.ShapeDtypeStruct((rows, depth), BF)] * count,
        compiler_params=params(),
        cost_estimate=cost(
            4 * count * rows * depth * hidden, 4 * count * depth * hidden + 4 * rows * hidden
        ),
        name="down_more",
    )(quarters, grad_gate, grad_up, *([gate_weight] * count), *([up_weight] * count))


def on_device(tokens, hidden_grad, routes, exponents, gate_weight, up_weight):
    etp = lax.axis_size("etp")
    experts = lax.axis_size("expert")
    own_rows, features = tokens.shape
    group_size = own_rows * etp
    capacity = 5 * group_size // (4 * experts)
    slots = experts * capacity
    x = lax.axis_index("etp").astype(jnp.int32)
    steps = jnp.arange(4, dtype=jnp.int32)
    ahead = (x + steps) % 4
    behind = (x - steps) % 4
    gate_w, up_w = gate_weight[0], up_weight[0]

    def back(array, r):
        return lax.ppermute(array, "etp", [(i, (i - r) % etp) for i in range(etp)])

    def forward(array, r):
        return lax.ppermute(array, "etp", [(i, (i + r) % etp) for i in range(etp)])

    with jax.named_scope("group_exchange"):
        own_routes = routes[:, 0]
        group_routes = jnp.concatenate([own_routes] + [back(own_routes, r) for r in (1, 2, 3)])
        token_parts = split_columns(tokens, behind)
        scales = jnp.exp2(exponents.astype(F32))[:, None]
        hidden_parts = split_columns(hidden_grad, behind, scales)
        group_tokens = jnp.concatenate(
            [token_parts[0]] + [back(token_parts[r], r) for r in (1, 2, 3)]
        )
        group_hidden = jnp.concatenate(
            [hidden_parts[0]] + [back(hidden_parts[r], r) for r in (1, 2, 3)]
        )

    with jax.named_scope("slots"):
        place = (ahead[:, None] * own_rows + jnp.arange(own_rows, dtype=jnp.int32)[None, :]).reshape(-1)
        earlier = (group_routes[:, None] == group_routes[None, :]) & (place[:, None] < place[None, :])
        rank = jnp.sum(earlier.astype(jnp.int32), axis=0)
        slot_index = group_routes * capacity + rank
        select = (jnp.arange(slots, dtype=jnp.int32)[:, None] == slot_index[None, :]).astype(BF)

    def pick(rows):
        return jnp.dot(select, rows, preferred_element_type=F32).astype(BF)

    def to_experts(array):
        return lax.all_to_all(array, "expert", split_axis=0, concat_axis=0, tiled=True)

    quarter = features // 4
    hidden = hidden_grad.shape[1] // 4
    with jax.named_scope("send_tokens"):
        packed_tokens = pick(group_tokens).reshape(experts, capacity // 2, 2, quarter)
        own_block = to_experts(packed_tokens).reshape(slots, quarter)
    with jax.named_scope("send_hidden"):
        packed_hidden = pick(group_hidden).reshape(experts, capacity * hidden // 128, 128)
        scaled = to_experts(packed_hidden).reshape(slots, hidden)

    with jax.named_scope("gather_width"):
        block1, block3, block2 = back(own_block, 1), back(own_block, 3), back(own_block, 2)
    with jax.named_scope("pre_activations"):
        order = jnp.stack([ahead[0], ahead[1], ahead[3], ahead[2]])
        gate, up = up_three((own_block, block1, block3), gate_w, up_w, order)
        for_gate, for_up = up_last(block2, gate, up, gate_w, up_w, order)
    with jax.named_scope("input_partials"):
        grad_gate, grad_up, part2 = down_first(scaled, for_gate, for_up, gate_w, up_w, ahead[2:3])
        part1, part3 = down_more(
            grad_gate, grad_up, gate_w, up_w, jnp.stack([ahead[1], ahead[3]]), 2
        )
        (part0,) = down_more(grad_gate, grad_up, gate_w, up_w, ahead[0:1], 1)
    with jax.named_scope("sum_quarters"):
        from2, from1, from3 = forward(part2, 2), forward(part1, 1), forward(part3, 3)
        summed = (
            part0.astype(F32) + from1.astype(F32) + from2.astype(F32) + from3.astype(F32)
        ).astype(BF)
    with jax.named_scope("return_tokens"):
        returned = to_experts(summed.reshape(experts, capacity // 2, 2, quarter))
        rows = returned.reshape(slots, quarter)
        group_rows = lax.dot_general(
            select, rows, (((0,), (0,)), ((), ())), preferred_element_type=F32
        ).astype(BF)
        parts = [group_rows[r * own_rows : (r + 1) * own_rows] for r in range(4)]
        blocks = [parts[0]] + [forward(parts[r], r) for r in (1, 2, 3)]
        return join_columns(blocks, behind)


def solution(mesh):
    placed = (
        P(("expert", "etp"), None),
        P(("expert", "etp"), None),
        P(("expert", "etp"), None),
        P(("expert", "etp")),
        P("expert", None, "etp"),
        P("expert", None, "etp"),
    )
    return jax.shard_map(
        on_device, mesh=mesh, in_specs=placed, out_specs=P(("expert", "etp"), None), check_vma=False
    )
```

```python
import jax
import jax.numpy as jnp
from jax import lax
from jax.experimental import pallas as pl
from jax.experimental.pallas import tpu as pltpu
from jax.sharding import PartitionSpec as P

BF = jnp.bfloat16
F32 = jnp.float32
VMEM_LIMIT = 20 * 1024 * 1024


def cost(flops, nbytes, trans=0):
    return pl.CostEstimate(flops=flops, bytes_accessed=nbytes, transcendentals=trans)


def params(grid_rank=1):
    return pltpu.CompilerParams(
        dimension_semantics=("arbitrary",) * grid_rank, vmem_limit_bytes=VMEM_LIMIT
    )


def in_hbm(array):
    return pltpu.with_memory_space_constraint(array, pltpu.HBM)


def quarter_at(x_ref, ahead):
    return (x_ref[0] + ahead) & 3


def split_columns(array, x, offsets, scale=None):
    rows, columns = array.shape
    width = columns // 4

    def kernel(x_ref, *refs):
        scale_refs = refs[4:-4]
        for source, target in zip(refs[:4], refs[-4:]):
            if scale_refs:
                target[...] = (source[...].astype(F32) * scale_refs[0][...]).astype(BF)
            else:
                target[...] = source[...]

    def block(offset):
        return pl.BlockSpec((rows, width), lambda i, x_ref: (0, quarter_at(x_ref, offset)))

    extra = [] if scale is None else [scale]
    return pl.pallas_call(
        kernel,
        grid_spec=pltpu.PrefetchScalarGridSpec(
            num_scalar_prefetch=1,
            grid=(1,),
            in_specs=[block(offset) for offset in offsets]
            + [pl.BlockSpec((rows, 1), lambda i, x_ref: (0, 0)) for _ in extra],
            out_specs=[pl.BlockSpec((rows, width), lambda i, x_ref: (0, 0))] * 4,
        ),
        out_shape=[jax.ShapeDtypeStruct((rows, width), BF)] * 4,
        compiler_params=params(),
        cost_estimate=cost(rows * columns, 4 * rows * columns),
        name="split_columns",
    )(x, array, array, array, array, *extra)


def join_columns(blocks, x, offsets):
    rows, width = blocks[0].shape

    def kernel(x_ref, b0, b1, b2, b3, out):
        for offset, block in zip(offsets, (b0, b1, b2, b3)):
            start = pl.multiple_of(quarter_at(x_ref, offset) * width, 128)
            out[:, pl.ds(start, width)] = block[...]

    return pl.pallas_call(
        kernel,
        grid_spec=pltpu.PrefetchScalarGridSpec(
            num_scalar_prefetch=1,
            grid=(1,),
            in_specs=[pl.BlockSpec((rows, width), lambda i, x_ref: (0, 0))] * 4,
            out_specs=pl.BlockSpec((rows, 4 * width), lambda i, x_ref: (0, 0)),
        ),
        out_shape=jax.ShapeDtypeStruct((rows, 4 * width), BF),
        compiler_params=params(),
        cost_estimate=cost(0, 16 * rows * width),
        name="join_columns",
    )(x, *blocks)


HIDDEN_TILE = 512


def up_three(blocks, offsets, gate_weight, up_weight, x):
    rows, depth = blocks[0].shape
    hidden = gate_weight.shape[1]

    def kernel(x_ref, t0, t1, t2, g0, g1, g2, u0, u1, u2, gate, up):
        for out, weights in ((gate, (g0, g1, g2)), (up, (u0, u1, u2))):
            total = jnp.dot(t0[...], weights[0][...], preferred_element_type=F32)
            total += jnp.dot(t1[...], weights[1][...], preferred_element_type=F32)
            total += jnp.dot(t2[...], weights[2][...], preferred_element_type=F32)
            out[...] = total

    def weight(offset):
        return pl.BlockSpec((depth, HIDDEN_TILE), lambda j, x_ref: (quarter_at(x_ref, offset), j))

    whole = pl.BlockSpec((rows, depth), lambda j, x_ref: (0, 0))
    out = pl.BlockSpec((rows, HIDDEN_TILE), lambda j, x_ref: (0, j))
    return pl.pallas_call(
        kernel,
        grid_spec=pltpu.PrefetchScalarGridSpec(
            num_scalar_prefetch=1,
            grid=(hidden // HIDDEN_TILE,),
            in_specs=[whole] * 3 + [weight(offset) for offset in offsets] * 2,
            out_specs=[out, out],
        ),
        out_shape=[pltpu.HBM((rows, hidden), F32)] * 2,
        compiler_params=params(),
        cost_estimate=cost(12 * rows * depth * hidden, 12 * depth * hidden + 8 * rows * hidden),
        name="up_three",
    )(x, *blocks, *([gate_weight] * 3), *([up_weight] * 3))


CONTRACT_LAST = (((1,), (1,)), ((), ()))


def down_dot(gg, gu, wg, wu):
    total = lax.dot_general(gg, wg, CONTRACT_LAST, preferred_element_type=F32)
    return total + lax.dot_general(gu, wu, CONTRACT_LAST, preferred_element_type=F32)


def middle(upper, lower, gate, up, scaled, offset, gate_weight, up_weight, x):
    half, depth = upper.shape
    rows, hidden = gate.shape
    steps = hidden // HIDDEN_TILE

    def kernel(x_ref, top, bottom, g_in, u_in, h, wg, wu, gg_out, gu_out, out_top, out_bottom, total):
        step = pl.program_id(0)
        for k, (t, out) in enumerate(((top, out_top), (bottom, out_bottom))):
            part = slice(k * half, (k + 1) * half)
            g = g_in[part, :] + jnp.dot(t[...], wg[...], preferred_element_type=F32)
            u = u_in[part, :] + jnp.dot(t[...], wu[...], preferred_element_type=F32)
            s = 1.0 / (1.0 + jnp.exp(-g))
            hs = h[part, :].astype(F32) * s
            gg = (hs * u * (1.0 + g * (1.0 - s))).astype(BF)
            gu = (hs * g).astype(BF)
            gg_out[part, :] = gg
            gu_out[part, :] = gu
            value = down_dot(gg, gu, wg[...], wu[...])

            @pl.when(step == 0)
            def _():
                total[part, :] = value

            @pl.when((step > 0) & (step < steps - 1))
            def _():
                total[part, :] += value

            @pl.when(step == steps - 1)
            def _():
                out[...] = (total[part, :] + value).astype(BF)

    weight = pl.BlockSpec((depth, HIDDEN_TILE), lambda j, x_ref: (quarter_at(x_ref, offset), j))
    tiled = pl.BlockSpec((rows, HIDDEN_TILE), lambda j, x_ref: (0, j))
    halves = [pl.BlockSpec((half, depth), lambda j, x_ref: (0, 0))] * 2
    return pl.pallas_call(
        kernel,
        grid_spec=pltpu.PrefetchScalarGridSpec(
            num_scalar_prefetch=1,
            grid=(steps,),
            in_specs=halves + [tiled] * 3 + [weight] * 2,
            out_specs=[tiled] * 2 + halves,
            scratch_shapes=[pltpu.VMEM((rows, depth), F32)],
        ),
        out_shape=[jax.ShapeDtypeStruct((rows, hidden), BF)] * 2
        + [jax.ShapeDtypeStruct((half, depth), BF)] * 2,
        compiler_params=params(),
        cost_estimate=cost(
            8 * rows * depth * hidden, 4 * depth * hidden + 14 * rows * hidden, rows * hidden
        ),
        name="middle",
    )(x, upper, lower, in_hbm(gate), in_hbm(up), scaled, gate_weight, up_weight)


def down_halves(grad_gate, grad_up, gate_weight, up_weight, x, pieces, dtype):
    rows, hidden = grad_gate.shape
    depth = gate_weight.shape[0] // 4
    half = rows // 2
    count = len(pieces)

    def at_step(j, values):
        chosen = values[0]
        for k in range(1, count):
            chosen = jnp.where(j == k, values[k], chosen)
        return chosen

    def kernel(x_ref, gg, gu, wg, wu, *outs):
        for k in range(count):

            @pl.when(pl.program_id(0) == k)
            def _():
                outs[k][...] = down_dot(gg[...], gu[...], wg[...], wu[...]).astype(dtype)

    weight = pl.BlockSpec(
        (depth, hidden),
        lambda j, x_ref: (quarter_at(x_ref, at_step(j, [offset for offset, _ in pieces])), 0),
    )
    grads = pl.BlockSpec((half, hidden), lambda j, x_ref: (at_step(j, [k for _, k in pieces]), 0))
    return pl.pallas_call(
        kernel,
        grid_spec=pltpu.PrefetchScalarGridSpec(
            num_scalar_prefetch=1,
            grid=(count,),
            in_specs=[grads] * 2 + [weight] * 2,
            out_specs=[pl.BlockSpec((half, depth), lambda j, x_ref: (0, 0))] * count,
        ),
        out_shape=[jax.ShapeDtypeStruct((half, depth), dtype)] * count,
        compiler_params=params(),
        cost_estimate=cost(
            4 * count * half * depth * hidden, 4 * count * depth * hidden + 4 * count * half * hidden
        ),
        name="down_halves",
    )(x, grad_gate, grad_up, gate_weight, up_weight)


def sum_halves(upper, lower):
    rows, width = upper[0].shape
    count = len(upper)

    def kernel(*refs):
        out = refs[-1]
        for k, half in enumerate((refs[:count], refs[count : 2 * count])):
            total = half[0][...].astype(F32)
            for ref in half[1:]:
                total = total + ref[...].astype(F32)
            out[k * rows : (k + 1) * rows, :] = total.astype(BF)

    return pl.pallas_call(
        kernel,
        out_shape=jax.ShapeDtypeStruct((2 * rows, width), BF),
        compiler_params=pltpu.CompilerParams(vmem_limit_bytes=VMEM_LIMIT),
        cost_estimate=cost(4 * rows * width, 16 * rows * width),
        name="sum_halves",
    )(*upper, *lower)


def on_device(tokens, hidden_grad, routes, exponents, gate_weight, up_weight):
    etp = lax.axis_size("etp")
    experts = lax.axis_size("expert")
    own_rows, features = tokens.shape
    group_size = own_rows * etp
    capacity = 5 * group_size // (4 * experts)
    slots = experts * capacity
    quarter, hidden = features // 4, hidden_grad.shape[1] // 4
    place_x = lax.axis_index("etp").astype(jnp.int32)
    x = place_x.reshape(1)
    gate_w, up_w = in_hbm(gate_weight[0]), in_hbm(up_weight[0])
    tokens, hidden_grad = in_hbm(tokens), in_hbm(hidden_grad)

    def back(array, r):
        return lax.ppermute(array, "etp", [(i, (i - r) % etp) for i in range(etp)])

    def forward(array, r):
        return lax.ppermute(array, "etp", [(i, (i + r) % etp) for i in range(etp)])

    ahead = (0, 2, 1, 3)
    with jax.named_scope("group_exchange"):
        token_parts = split_columns(tokens, x, [-r for r in ahead])
        group_tokens = jnp.concatenate(
            [token_parts[0]] + [back(token_parts[k], ahead[k]) for k in (1, 2, 3)]
        )
        own_routes = routes[:, 0]
        group_routes = jnp.concatenate([own_routes] + [back(own_routes, r) for r in ahead[1:]])
        scales = jnp.exp2(exponents.astype(F32))[:, None]
        hidden_parts = split_columns(hidden_grad, x, [-r for r in ahead], scales)
        group_hidden = jnp.concatenate(
            [hidden_parts[0]] + [back(hidden_parts[k], ahead[k]) for k in (1, 2, 3)]
        )

    with jax.named_scope("slots"):
        row = jnp.arange(group_size, dtype=jnp.int32)
        block = row // own_rows
        offset = jnp.where(block == 1, 2, jnp.where(block == 2, 1, block))
        place = ((place_x + offset) & 3) * own_rows + row % own_rows
        earlier = (group_routes[:, None] == group_routes[None, :]) & (place[:, None] < place[None, :])
        rank = jnp.sum(earlier.astype(jnp.int32), axis=0)
        slot_index = group_routes * capacity + rank
        select = (jnp.arange(slots, dtype=jnp.int32)[:, None] == slot_index[None, :]).astype(BF)

    def pick(rows):
        return jnp.dot(select, rows, preferred_element_type=F32).astype(BF)

    def to_experts(array):
        return lax.all_to_all(array, "expert", split_axis=0, concat_axis=0, tiled=True)

    with jax.named_scope("send_tokens"):
        packed_tokens = pick(group_tokens).reshape(experts, capacity // 2, 2, quarter)
        own_block = to_experts(packed_tokens).reshape(slots, quarter)
    with jax.named_scope("send_hidden"):
        packed_hidden = pick(group_hidden).reshape(experts, capacity * hidden // 128, 128)
        scaled = to_experts(packed_hidden).reshape(slots, hidden)

    half = slots // 2
    with jax.named_scope("gather_width"):
        left_block, right_block = forward(own_block, 1), back(own_block, 1)
        far_upper, far_lower = forward(left_block[:half], 1), back(right_block[half:], 1)
    with jax.named_scope("pre_activations"):
        gate, up = up_three((own_block, right_block, left_block), (0, 1, 3), gate_w, up_w, x)
    with jax.named_scope("input_partials"):
        grad_gate, grad_up, far_top, far_bottom = middle(
            far_upper, far_lower, gate, up, scaled, 2, gate_w, up_w, x
        )
        right_bottom, left_top = down_halves(
            grad_gate, grad_up, gate_w, up_w, x, ((1, 1), (3, 0)), BF
        )
        right_top, left_bottom = down_halves(
            grad_gate, grad_up, gate_w, up_w, x, ((1, 0), (3, 1)), F32
        )
        own_top, own_bottom = down_halves(
            grad_gate, grad_up, gate_w, up_w, x, ((0, 0), (0, 1)), F32
        )
    with jax.named_scope("sum_quarters"):
        passed_top, passed_bottom = forward(far_top, 1), back(far_bottom, 1)
        from_left_bottom, from_right_top = forward(right_bottom, 1), back(left_top, 1)
        from_left_top = forward((right_top + passed_top.astype(F32)).astype(BF), 1)
        from_right_bottom = back((left_bottom + passed_bottom.astype(F32)).astype(BF), 1)
        summed = sum_halves(
            (own_top, from_left_top, from_right_top),
            (own_bottom, from_left_bottom, from_right_bottom),
        )
    with jax.named_scope("return_tokens"):
        returned = to_experts(summed.reshape(experts, capacity // 2, 2, quarter))
        rows = returned.reshape(slots, quarter)
        group_rows = lax.dot_general(
            select, rows, (((0,), (0,)), ((), ())), preferred_element_type=F32
        ).astype(BF)
        parts = [group_rows[k * own_rows : (k + 1) * own_rows] for k in range(4)]
        blocks = [parts[0]] + [forward(parts[k], ahead[k]) for k in (1, 2, 3)]
        return join_columns(blocks, x, [-r for r in ahead])


def solution(mesh):
    placed = (
        P(("expert", "etp"), None),
        P(("expert", "etp"), None),
        P(("expert", "etp"), None),
        P(("expert", "etp")),
        P("expert", None, "etp"),
        P("expert", None, "etp"),
    )
    return jax.shard_map(
        on_device, mesh=mesh, in_specs=placed, out_specs=P(("expert", "etp"), None), check_vma=False
    )
```

```python
import jax
import jax.numpy as jnp
from jax import lax
from jax.experimental import pallas as pl
from jax.experimental.pallas import tpu as pltpu
from jax.sharding import PartitionSpec as P

BF = jnp.bfloat16
F32 = jnp.float32
VMEM_LIMIT = 20 * 1024 * 1024


def cost(flops, nbytes, trans=0):
    return pl.CostEstimate(flops=flops, bytes_accessed=nbytes, transcendentals=trans)


def params(grid_rank=1):
    return pltpu.CompilerParams(
        dimension_semantics=("arbitrary",) * grid_rank, vmem_limit_bytes=VMEM_LIMIT
    )


def in_hbm(array):
    return pltpu.with_memory_space_constraint(array, pltpu.HBM)


def quarter_at(x_ref, ahead):
    return (x_ref[0] + ahead) & 3


def split_columns(array, x, offsets, scale=None):
    rows, columns = array.shape
    width = columns // 4

    def kernel(x_ref, *refs):
        scale_refs = refs[4:-4]
        for source, target in zip(refs[:4], refs[-4:]):
            if scale_refs:
                target[...] = (source[...].astype(F32) * scale_refs[0][...]).astype(BF)
            else:
                target[...] = source[...]

    def block(offset):
        return pl.BlockSpec((rows, width), lambda i, x_ref: (0, quarter_at(x_ref, offset)))

    extra = [] if scale is None else [scale]
    return pl.pallas_call(
        kernel,
        grid_spec=pltpu.PrefetchScalarGridSpec(
            num_scalar_prefetch=1,
            grid=(1,),
            in_specs=[block(offset) for offset in offsets]
            + [pl.BlockSpec((rows, 1), lambda i, x_ref: (0, 0)) for _ in extra],
            out_specs=[pl.BlockSpec((rows, width), lambda i, x_ref: (0, 0))] * 4,
        ),
        out_shape=[jax.ShapeDtypeStruct((rows, width), BF)] * 4,
        compiler_params=params(),
        cost_estimate=cost(rows * columns, 4 * rows * columns),
        name="split_columns",
    )(x, array, array, array, array, *extra)


def join_columns(blocks, x, offsets):
    rows, width = blocks[0].shape

    def kernel(x_ref, b0, b1, b2, b3, out):
        for offset, block in zip(offsets, (b0, b1, b2, b3)):
            start = pl.multiple_of(quarter_at(x_ref, offset) * width, 128)
            out[:, pl.ds(start, width)] = block[...]

    return pl.pallas_call(
        kernel,
        grid_spec=pltpu.PrefetchScalarGridSpec(
            num_scalar_prefetch=1,
            grid=(1,),
            in_specs=[pl.BlockSpec((rows, width), lambda i, x_ref: (0, 0))] * 4,
            out_specs=pl.BlockSpec((rows, 4 * width), lambda i, x_ref: (0, 0)),
        ),
        out_shape=jax.ShapeDtypeStruct((rows, 4 * width), BF),
        compiler_params=params(),
        cost_estimate=cost(0, 16 * rows * width),
        name="join_columns",
    )(x, *blocks)


def slot_matrix(route_blocks, x, offsets, experts, capacity):
    own_rows = route_blocks[0].shape[1]
    group = own_rows * len(offsets)
    slots = experts * capacity

    def kernel(x_ref, r0, r1, r2, r3, out):
        routes = jnp.concatenate([r[...] for r in (r0, r1, r2, r3)], axis=1)

        def places(axis):
            row = lax.broadcasted_iota(jnp.int32, (group, group), axis)
            block = row // own_rows
            offset = jnp.zeros_like(row)
            for k, value in enumerate(offsets):
                offset = jnp.where(block == k, value, offset)
            return ((x_ref[0] + offset) & 3) * own_rows + row % own_rows

        before = jnp.where(places(0) < places(1), 1.0, 0.0).astype(BF)
        same = lax.broadcasted_iota(jnp.int32, (experts, group), 0) == routes
        named = jnp.where(same, 1.0, 0.0)
        counts = jnp.dot(named.astype(BF), before, preferred_element_type=F32)
        rank = jnp.sum(named * counts, axis=0, keepdims=True).astype(jnp.int32)
        slot = routes * capacity + rank
        filled = lax.broadcasted_iota(jnp.int32, (slots, group), 0) == slot
        out[...] = jnp.where(filled, 1.0, 0.0).astype(BF)

    block = pl.BlockSpec((1, own_rows), lambda i, x_ref: (0, 0))
    return pl.pallas_call(
        kernel,
        grid_spec=pltpu.PrefetchScalarGridSpec(
            num_scalar_prefetch=1,
            grid=(1,),
            in_specs=[block] * 4,
            out_specs=pl.BlockSpec((slots, group), lambda i, x_ref: (0, 0)),
        ),
        out_shape=jax.ShapeDtypeStruct((slots, group), BF),
        compiler_params=params(),
        cost_estimate=cost(0, 0),
        name="slot_matrix",
    )(x, *route_blocks)


HIDDEN_TILE = 512


def up_sums(uppers, lowers, offsets, gate_weight, up_weight, x, so_far=()):
    half, depth = uppers[0].shape
    hidden = gate_weight.shape[1]
    rows, count = 2 * half, len(offsets)
    tile = 256

    def kernel(x_ref, *refs):
        gate, up = refs[-2:]
        starts = refs[4 * count : -2]
        for k in range(2):
            part = slice(k * half, (k + 1) * half)
            blocks = refs[k * count : (k + 1) * count]
            for n, out in enumerate((gate, up)):
                weights = refs[(2 + n) * count : (3 + n) * count]
                total = jnp.dot(blocks[0][...], weights[0][...], preferred_element_type=F32)
                for block, w in zip(blocks[1:], weights[1:]):
                    total += jnp.dot(block[...], w[...], preferred_element_type=F32)
                if starts:
                    total += starts[n][part, :]
                out[part, :] = total

    def weight(offset):
        return pl.BlockSpec((depth, tile), lambda j, x_ref: (quarter_at(x_ref, offset), j))

    tiled = pl.BlockSpec((rows, tile), lambda j, x_ref: (0, j))
    return pl.pallas_call(
        kernel,
        grid_spec=pltpu.PrefetchScalarGridSpec(
            num_scalar_prefetch=1,
            grid=(hidden // tile,),
            in_specs=[pl.BlockSpec((half, depth), lambda j, x_ref: (0, 0))] * (2 * count)
            + [weight(offset) for offset in offsets] * 2
            + [tiled] * len(so_far),
            out_specs=[tiled, tiled],
        ),
        out_shape=[pltpu.HBM((rows, hidden), F32)] * 2,
        compiler_params=params(),
        cost_estimate=cost(
            4 * count * rows * depth * hidden, 4 * count * depth * hidden + 16 * rows * hidden
        ),
        name="up_sums",
    )(
        x,
        *uppers,
        *lowers,
        *([gate_weight] * count),
        *([up_weight] * count),
        *(in_hbm(array) for array in so_far),
    )


CONTRACT_LAST = (((1,), (1,)), ((), ()))


def down_dot(gg, gu, wg, wu):
    total = lax.dot_general(gg, wg, CONTRACT_LAST, preferred_element_type=F32)
    return total + lax.dot_general(gu, wu, CONTRACT_LAST, preferred_element_type=F32)


def middle(upper, lower, gate, up, scaled, offset, gate_weight, up_weight, x):
    half, depth = upper.shape
    rows, hidden = gate.shape
    steps = hidden // HIDDEN_TILE

    def kernel(x_ref, top, bottom, g_in, u_in, h, wg, wu, gg_out, gu_out, out_top, out_bottom, total):
        step = pl.program_id(0)
        for k, (t, out) in enumerate(((top, out_top), (bottom, out_bottom))):
            part = slice(k * half, (k + 1) * half)
            g = g_in[part, :] + jnp.dot(t[...], wg[...], preferred_element_type=F32)
            u = u_in[part, :] + jnp.dot(t[...], wu[...], preferred_element_type=F32)
            s = 1.0 / (1.0 + jnp.exp(-g))
            hs = h[part, :].astype(F32) * s
            gg = (hs * u * (1.0 + g * (1.0 - s))).astype(BF)
            gu = (hs * g).astype(BF)
            gg_out[part, :] = gg
            gu_out[part, :] = gu
            value = down_dot(gg, gu, wg[...], wu[...])

            @pl.when(step == 0)
            def _():
                total[part, :] = value

            @pl.when((step > 0) & (step < steps - 1))
            def _():
                total[part, :] += value

            @pl.when(step == steps - 1)
            def _():
                out[...] = (total[part, :] + value).astype(BF)

    weight = pl.BlockSpec((depth, HIDDEN_TILE), lambda j, x_ref: (quarter_at(x_ref, offset), j))
    tiled = pl.BlockSpec((rows, HIDDEN_TILE), lambda j, x_ref: (0, j))
    halves = [pl.BlockSpec((half, depth), lambda j, x_ref: (0, 0))] * 2
    return pl.pallas_call(
        kernel,
        grid_spec=pltpu.PrefetchScalarGridSpec(
            num_scalar_prefetch=1,
            grid=(steps,),
            in_specs=halves + [tiled] * 3 + [weight] * 2,
            out_specs=[tiled] * 2 + halves,
            scratch_shapes=[pltpu.VMEM((rows, depth), F32)],
        ),
        out_shape=[jax.ShapeDtypeStruct((rows, hidden), BF)] * 2
        + [jax.ShapeDtypeStruct((half, depth), BF)] * 2,
        compiler_params=params(),
        cost_estimate=cost(
            8 * rows * depth * hidden, 4 * depth * hidden + 14 * rows * hidden, rows * hidden
        ),
        name="middle",
    )(x, upper, lower, in_hbm(gate), in_hbm(up), scaled, gate_weight, up_weight)


def down_halves(grad_gate, grad_up, gate_weight, up_weight, x, pieces, dtype):
    rows, hidden = grad_gate.shape
    depth = gate_weight.shape[0] // 4
    half = rows // 2
    count = len(pieces)

    def at_step(j, values):
        chosen = values[0]
        for k in range(1, count):
            chosen = jnp.where(j == k, values[k], chosen)
        return chosen

    def kernel(x_ref, gg, gu, wg, wu, *outs):
        for k in range(count):

            @pl.when(pl.program_id(0) == k)
            def _():
                outs[k][...] = down_dot(gg[...], gu[...], wg[...], wu[...]).astype(dtype)

    weight = pl.BlockSpec(
        (depth, hidden),
        lambda j, x_ref: (quarter_at(x_ref, at_step(j, [offset for offset, _ in pieces])), 0),
    )
    grads = pl.BlockSpec((half, hidden), lambda j, x_ref: (at_step(j, [k for _, k in pieces]), 0))
    return pl.pallas_call(
        kernel,
        grid_spec=pltpu.PrefetchScalarGridSpec(
            num_scalar_prefetch=1,
            grid=(count,),
            in_specs=[grads] * 2 + [weight] * 2,
            out_specs=[pl.BlockSpec((half, depth), lambda j, x_ref: (0, 0))] * count,
        ),
        out_shape=[jax.ShapeDtypeStruct((half, depth), dtype)] * count,
        compiler_params=params(),
        cost_estimate=cost(
            1 * count * half * depth * hidden, 4 * count * depth * hidden + 4 * count * half * hidden
        ),
        name="down_halves",
    )(x, grad_gate, grad_up, gate_weight, up_weight)


def sum_halves(upper, lower):
    rows, width = upper[0].shape
    count = len(upper)

    def kernel(*refs):
        out = refs[-1]
        for k, half in enumerate((refs[:count], refs[count : 2 * count])):
            total = half[0][...].astype(F32)
            for ref in half[1:]:
                total = total + ref[...].astype(F32)
            out[k * rows : (k + 1) * rows, :] = total.astype(BF)

    return pl.pallas_call(
        kernel,
        out_shape=jax.ShapeDtypeStruct((2 * rows, width), BF),
        compiler_params=pltpu.CompilerParams(vmem_limit_bytes=VMEM_LIMIT),
        cost_estimate=cost(4 * rows * width, 16 * rows * width),
        name="sum_halves",
    )(*upper, *lower)


def on_device(tokens, hidden_grad, routes, exponents, gate_weight, up_weight):
    etp = lax.axis_size("etp")
    experts = lax.axis_size("expert")
    own_rows, features = tokens.shape
    capacity = 5 * own_rows * etp // (4 * experts)
    slots = experts * capacity
    quarter, hidden = features // 4, hidden_grad.shape[1] // 4
    x = lax.axis_index("etp").astype(jnp.int32).reshape(1)
    gate_w, up_w = in_hbm(gate_weight[0]), in_hbm(up_weight[0])
    tokens, hidden_grad = in_hbm(tokens), in_hbm(hidden_grad)

    def back(array, r):
        return lax.ppermute(array, "etp", [(i, (i - r) % etp) for i in range(etp)])

    def forward(array, r):
        return lax.ppermute(array, "etp", [(i, (i + r) % etp) for i in range(etp)])

    ahead = (0, 2, 1, 3)
    with jax.named_scope("group_exchange"):
        token_parts = split_columns(tokens, x, [-r for r in ahead])
        group_tokens = jnp.concatenate(
            [token_parts[0]] + [back(token_parts[k], ahead[k]) for k in (1, 2, 3)]
        )
        own_routes = routes.reshape(1, own_rows)
        route_blocks = [own_routes] + [back(own_routes, r) for r in ahead[1:]]
        scales = jnp.exp2(exponents.astype(F32))[:, None]
        hidden_parts = split_columns(hidden_grad, x, [-r for r in ahead], scales)
        group_hidden = jnp.concatenate(
            [hidden_parts[0]] + [back(hidden_parts[k], ahead[k]) for k in (1, 2, 3)]
        )

    with jax.named_scope("slots"):
        select = slot_matrix(route_blocks, x, ahead, experts, capacity)

    def pick(rows):
        return jnp.dot(select, rows, preferred_element_type=F32).astype(BF)

    def to_experts(array):
        return lax.all_to_all(array, "expert", split_axis=0, concat_axis=0, tiled=True)

    with jax.named_scope("send_tokens"):
        packed_tokens = pick(group_tokens).reshape(experts, capacity // 2, 2, quarter)
        arrived = to_experts(packed_tokens)
        top = arrived[: experts // 2].reshape(slots // 2, quarter)
        bottom = arrived[experts // 2 :].reshape(slots // 2, quarter)
    with jax.named_scope("send_hidden"):
        packed_hidden = pick(group_hidden).reshape(experts, capacity * hidden // 128, 128)
        scaled = to_experts(packed_hidden).reshape(slots, hidden)

    with jax.named_scope("gather_width"):
        own_sums = up_sums((top,), (bottom,), (0,), gate_w, up_w, x)
        left_top, right_bottom, *own_sums = lax.optimization_barrier(
            (forward(top, 1), back(bottom, 1), *own_sums)
        )
        far_upper, far_lower = forward(left_top, 1), back(right_bottom, 1)
        left_bottom, right_top = forward(bottom, 1), back(top, 1)
    with jax.named_scope("pre_activations"):
        gate, up = up_sums(
            (right_top, left_top), (right_bottom, left_bottom), (1, 3), gate_w, up_w, x, own_sums
        )
    with jax.named_scope("input_partials"):
        grad_gate, grad_up, far_top, far_bottom = middle(
            far_upper, far_lower, gate, up, scaled, 2, gate_w, up_w, x
        )
        right_bottom, left_top = down_halves(
            grad_gate, grad_up, gate_w, up_w, x, ((1, 1), (3, 0)), BF
        )
        right_top, left_bottom = down_halves(
            grad_gate, grad_up, gate_w, up_w, x, ((1, 0), (3, 1)), F32
        )
        own_top, own_bottom = down_halves(
            grad_gate, grad_up, gate_w, up_w, x, ((0, 0), (0, 1)), F32
        )
    with jax.named_scope("sum_quarters"):
        passed_top, passed_bottom = forward(far_top, 1), back(far_bottom, 1)
        from_left_bottom, from_right_top = forward(right_bottom, 1), back(left_top, 1)
        from_left_top = forward((right_top + passed_top.astype(F32)).astype(BF), 1)
        from_right_bottom = back((left_bottom + passed_bottom.astype(F32)).astype(BF), 1)
        summed = sum_halves(
            (own_top, from_left_top, from_right_top),
            (own_bottom, from_left_bottom, from_right_bottom),
        )
    with jax.named_scope("return_tokens"):
        returned = to_experts(summed.reshape(experts, capacity // 2, 2, quarter))
        rows = returned.reshape(slots, quarter)
        group_rows = lax.dot_general(
            select, rows, (((0,), (0,)), ((), ())), preferred_element_type=F32
        ).astype(BF)
        parts = [group_rows[k * own_rows : (k + 1) * own_rows] for k in range(4)]
        blocks = [parts[0]] + [forward(parts[k], ahead[k]) for k in (1, 2, 3)]
        return join_columns(blocks, x, [-r for r in ahead])


def solution(mesh):
    placed = (
        P(("expert", "etp"), None),
        P(("expert", "etp"), None),
        P(("expert", "etp"), None),
        P(("expert", "etp")),
        P("expert", None, "etp"),
        P("expert", None, "etp"),
    )
    return jax.shard_map(
        on_device, mesh=mesh, in_specs=placed, out_specs=P(("expert", "etp"), None), check_vma=False
    )
```

```python
import jax
import jax.numpy as jnp
from jax import lax
from jax.experimental import pallas as pl
from jax.experimental.pallas import tpu as pltpu
from jax.sharding import PartitionSpec as P

BF = jnp.bfloat16
F32 = jnp.float32
VMEM_LIMIT = 20 * 1024 * 1024


def cost(flops, nbytes, trans=0):
    return pl.CostEstimate(flops=flops, bytes_accessed=nbytes, transcendentals=trans)


def params(grid_rank=1):
    return pltpu.CompilerParams(
        dimension_semantics=("arbitrary",) * grid_rank, vmem_limit_bytes=VMEM_LIMIT
    )


def in_hbm(array):
    return pltpu.with_memory_space_constraint(array, pltpu.HBM)


def quarter_at(x_ref, ahead):
    return (x_ref[0] + ahead) & 3


def split_columns(array, x, offsets, scale=None):
    rows, columns = array.shape
    width = columns // 4

    def kernel(x_ref, *refs):
        scale_refs = refs[4:-4]
        for source, target in zip(refs[:4], refs[-4:]):
            if scale_refs:
                target[...] = (source[...].astype(F32) * scale_refs[0][...]).astype(BF)
            else:
                target[...] = source[...]

    def block(offset):
        return pl.BlockSpec((rows, width), lambda i, x_ref: (0, quarter_at(x_ref, offset)))

    extra = [] if scale is None else [scale]
    return pl.pallas_call(
        kernel,
        grid_spec=pltpu.PrefetchScalarGridSpec(
            num_scalar_prefetch=1,
            grid=(1,),
            in_specs=[block(offset) for offset in offsets]
            + [pl.BlockSpec((rows, 1), lambda i, x_ref: (0, 0)) for _ in extra],
            out_specs=[pl.BlockSpec((rows, width), lambda i, x_ref: (0, 0))] * 4,
        ),
        out_shape=[jax.ShapeDtypeStruct((rows, width), BF)] * 4,
        compiler_params=params(),
        cost_estimate=cost(rows * columns, 4 * rows * columns),
        name="split_columns",
    )(x, array, array, array, array, *extra)


def join_columns(blocks, x, offsets):
    rows, width = blocks[0].shape

    def kernel(x_ref, b0, b1, b2, b3, out):
        for offset, block in zip(offsets, (b0, b1, b2, b3)):
            start = pl.multiple_of(quarter_at(x_ref, offset) * width, 128)
            out[:, pl.ds(start, width)] = block[...]

    return pl.pallas_call(
        kernel,
        grid_spec=pltpu.PrefetchScalarGridSpec(
            num_scalar_prefetch=1,
            grid=(1,),
            in_specs=[pl.BlockSpec((rows, width), lambda i, x_ref: (0, 0))] * 4,
            out_specs=pl.BlockSpec((rows, 4 * width), lambda i, x_ref: (0, 0)),
        ),
        out_shape=jax.ShapeDtypeStruct((rows, 4 * width), BF),
        compiler_params=params(),
        cost_estimate=cost(0, 16 * rows * width),
        name="join_columns",
    )(x, *blocks)


def slot_matrix(route_blocks, x, offsets, experts, capacity):
    own_rows = route_blocks[0].shape[1]
    group = own_rows * len(offsets)
    slots = experts * capacity

    def kernel(x_ref, r0, r1, r2, r3, out):
        routes = jnp.concatenate([r[...] for r in (r0, r1, r2, r3)], axis=1)

        def places(axis):
            row = lax.broadcasted_iota(jnp.int32, (group, group), axis)
            block = row // own_rows
            offset = jnp.zeros_like(row)
            for k, value in enumerate(offsets):
                offset = jnp.where(block == k, value, offset)
            return ((x_ref[0] + offset) & 3) * own_rows + row % own_rows

        before = jnp.where(places(0) < places(1), 1.0, 0.0).astype(BF)
        same = lax.broadcasted_iota(jnp.int32, (experts, group), 0) == routes
        named = jnp.where(same, 1.0, 0.0)
        counts = jnp.dot(named.astype(BF), before, preferred_element_type=F32)
        rank = jnp.sum(named * counts, axis=0, keepdims=True).astype(jnp.int32)
        slot = routes * capacity + rank
        filled = lax.broadcasted_iota(jnp.int32, (slots, group), 0) == slot
        out[...] = jnp.where(filled, 1.0, 0.0).astype(BF)

    block = pl.BlockSpec((1, own_rows), lambda i, x_ref: (0, 0))
    return pl.pallas_call(
        kernel,
        grid_spec=pltpu.PrefetchScalarGridSpec(
            num_scalar_prefetch=1,
            grid=(1,),
            in_specs=[block] * 4,
            out_specs=pl.BlockSpec((slots, group), lambda i, x_ref: (0, 0)),
        ),
        out_shape=jax.ShapeDtypeStruct((slots, group), BF),
        compiler_params=params(),
        cost_estimate=cost(0, 0),
        name="slot_matrix",
    )(x, *route_blocks)


HIDDEN_TILE = 512
SCHEDULE_WEIGHT = 6


def up_sums(blocks, offsets, gate_weight, up_weight, x, so_far=()):
    rows, depth = blocks[0].shape
    hidden = gate_weight.shape[1]
    count = len(offsets)

    def kernel(x_ref, *refs):
        starts = refs[3 * count : -2]
        for n, out in enumerate(refs[-2:]):
            weights = refs[(1 + n) * count : (2 + n) * count]
            total = jnp.dot(refs[0][...], weights[0][...], preferred_element_type=F32)
            for block, w in zip(refs[1:count], weights[1:]):
                total += jnp.dot(block[...], w[...], preferred_element_type=F32)
            if starts:
                total += starts[n][...]
            out[...] = total

    def weight(offset):
        return pl.BlockSpec((depth, HIDDEN_TILE), lambda j, x_ref: (quarter_at(x_ref, offset), j))

    tiled = pl.BlockSpec((rows, HIDDEN_TILE), lambda j, x_ref: (0, j))
    if so_far:
        out_shape = [pltpu.HBM((rows, hidden), F32)] * 2
    else:
        out_shape = [jax.ShapeDtypeStruct((rows, hidden), F32)] * 2
    return pl.pallas_call(
        kernel,
        grid_spec=pltpu.PrefetchScalarGridSpec(
            num_scalar_prefetch=1,
            grid=(hidden // HIDDEN_TILE,),
            in_specs=[pl.BlockSpec((rows, depth), lambda j, x_ref: (0, 0))] * count
            + [weight(offset) for offset in offsets] * 2
            + [tiled] * len(so_far),
            out_specs=[tiled, tiled],
        ),
        out_shape=out_shape,
        compiler_params=params(),
        cost_estimate=cost(
            SCHEDULE_WEIGHT * 4 * count * rows * depth * hidden, 4 * count * depth * hidden + 16 * rows * hidden
        ),
        name="up_sums",
    )(x, *blocks, *([gate_weight] * count), *([up_weight] * count), *so_far)


CONTRACT_LAST = (((1,), (1,)), ((), ()))


def down_dot(gg, gu, wg, wu):
    total = lax.dot_general(gg, wg, CONTRACT_LAST, preferred_element_type=F32)
    return total + lax.dot_general(gu, wu, CONTRACT_LAST, preferred_element_type=F32)


def up_last(upper, lower, gate, up, offset, gate_weight, up_weight, x):
    half, depth = upper.shape
    rows, hidden = gate.shape

    def kernel(x_ref, top, bottom, g_in, u_in, wg, wu, for_gate, for_up):
        for k, t in enumerate((top, bottom)):
            part = slice(k * half, (k + 1) * half)
            g = g_in[part, :] + jnp.dot(t[...], wg[...], preferred_element_type=F32)
            u = u_in[part, :] + jnp.dot(t[...], wu[...], preferred_element_type=F32)
            s = 1.0 / (1.0 + jnp.exp(-g))
            for_gate[part, :] = u * s * (1.0 + g * (1.0 - s))
            for_up[part, :] = g * s

    weight = pl.BlockSpec((depth, HIDDEN_TILE), lambda j, x_ref: (quarter_at(x_ref, offset), j))
    tiled = pl.BlockSpec((rows, HIDDEN_TILE), lambda j, x_ref: (0, j))
    halves = [pl.BlockSpec((half, depth), lambda j, x_ref: (0, 0))] * 2
    return pl.pallas_call(
        kernel,
        grid_spec=pltpu.PrefetchScalarGridSpec(
            num_scalar_prefetch=1,
            grid=(hidden // HIDDEN_TILE,),
            in_specs=halves + [tiled] * 2 + [weight] * 2,
            out_specs=[tiled] * 2,
        ),
        out_shape=[pltpu.HBM((rows, hidden), F32)] * 2,
        compiler_params=params(),
        cost_estimate=cost(
            4 * rows * depth * hidden, 4 * depth * hidden + 16 * rows * hidden, rows * hidden
        ),
        name="up_last",
    )(x, upper, lower, gate, up, gate_weight, up_weight)


def down_first(scaled, for_gate, for_up, offset, gate_weight, up_weight, x):
    rows, hidden = scaled.shape
    depth = gate_weight.shape[0] // 4
    half = rows // 2
    steps = hidden // HIDDEN_TILE

    def kernel(x_ref, h, a, b, wg, wu, gg_out, gu_out, out_top, out_bottom, total):
        step = pl.program_id(0)
        for k, out in enumerate((out_top, out_bottom)):
            part = slice(k * half, (k + 1) * half)
            h_part = h[part, :].astype(F32)
            gg = (h_part * a[part, :]).astype(BF)
            gu = (h_part * b[part, :]).astype(BF)
            gg_out[part, :] = gg
            gu_out[part, :] = gu
            value = down_dot(gg, gu, wg[...], wu[...])

            @pl.when(step == 0)
            def _():
                total[part, :] = value

            @pl.when((step > 0) & (step < steps - 1))
            def _():
                total[part, :] += value

            @pl.when(step == steps - 1)
            def _():
                out[...] = (total[part, :] + value).astype(BF)

    weight = pl.BlockSpec((depth, HIDDEN_TILE), lambda j, x_ref: (quarter_at(x_ref, offset), j))
    tiled = pl.BlockSpec((rows, HIDDEN_TILE), lambda j, x_ref: (0, j))
    halves = [pl.BlockSpec((half, depth), lambda j, x_ref: (0, 0))] * 2
    return pl.pallas_call(
        kernel,
        grid_spec=pltpu.PrefetchScalarGridSpec(
            num_scalar_prefetch=1,
            grid=(steps,),
            in_specs=[tiled] * 3 + [weight] * 2,
            out_specs=[tiled] * 2 + halves,
            scratch_shapes=[pltpu.VMEM((rows, depth), F32)],
        ),
        out_shape=[jax.ShapeDtypeStruct((rows, hidden), BF)] * 2
        + [jax.ShapeDtypeStruct((half, depth), BF)] * 2,
        compiler_params=params(),
        cost_estimate=cost(4 * rows * depth * hidden, 4 * depth * hidden + 14 * rows * hidden),
        name="down_first",
    )(x, scaled, in_hbm(for_gate), in_hbm(for_up), gate_weight, up_weight)


def down_halves(grad_gate, grad_up, gate_weight, up_weight, x, pieces, dtype):
    rows, hidden = grad_gate.shape
    depth = gate_weight.shape[0] // 4
    half = rows // 2
    count = len(pieces)

    def at_step(j, values):
        chosen = values[0]
        for k in range(1, count):
            chosen = jnp.where(j == k, values[k], chosen)
        return chosen

    def kernel(x_ref, gg, gu, wg, wu, *outs):
        for k in range(count):

            @pl.when(pl.program_id(0) == k)
            def _():
                outs[k][...] = down_dot(gg[...], gu[...], wg[...], wu[...]).astype(dtype)

    weight = pl.BlockSpec(
        (depth, hidden),
        lambda j, x_ref: (quarter_at(x_ref, at_step(j, [offset for offset, _ in pieces])), 0),
    )
    grads = pl.BlockSpec((half, hidden), lambda j, x_ref: (at_step(j, [k for _, k in pieces]), 0))
    return pl.pallas_call(
        kernel,
        grid_spec=pltpu.PrefetchScalarGridSpec(
            num_scalar_prefetch=1,
            grid=(count,),
            in_specs=[grads] * 2 + [weight] * 2,
            out_specs=[pl.BlockSpec((half, depth), lambda j, x_ref: (0, 0))] * count,
        ),
        out_shape=[jax.ShapeDtypeStruct((half, depth), dtype)] * count,
        compiler_params=params(),
        cost_estimate=cost(
            1 * count * half * depth * hidden, 4 * count * depth * hidden + 4 * count * half * hidden
        ),
        name="down_halves",
    )(x, grad_gate, grad_up, gate_weight, up_weight)


def sum_halves(upper, lower):
    rows, width = upper[0].shape
    count = len(upper)

    def kernel(*refs):
        out = refs[-1]
        for k, half in enumerate((refs[:count], refs[count : 2 * count])):
            total = half[0][...].astype(F32)
            for ref in half[1:]:
                total = total + ref[...].astype(F32)
            out[k * rows : (k + 1) * rows, :] = total.astype(BF)

    return pl.pallas_call(
        kernel,
        out_shape=jax.ShapeDtypeStruct((2 * rows, width), BF),
        compiler_params=pltpu.CompilerParams(vmem_limit_bytes=VMEM_LIMIT),
        cost_estimate=cost(4 * rows * width, 16 * rows * width),
        name="sum_halves",
    )(*upper, *lower)


def on_device(tokens, hidden_grad, routes, exponents, gate_weight, up_weight):
    etp = lax.axis_size("etp")
    experts = lax.axis_size("expert")
    own_rows, features = tokens.shape
    capacity = 5 * own_rows * etp // (4 * experts)
    slots = experts * capacity
    quarter, hidden = features // 4, hidden_grad.shape[1] // 4
    x = lax.axis_index("etp").astype(jnp.int32).reshape(1)
    gate_w, up_w = in_hbm(gate_weight[0]), in_hbm(up_weight[0])
    tokens, hidden_grad = in_hbm(tokens), in_hbm(hidden_grad)

    def back(array, r):
        return lax.ppermute(array, "etp", [(i, (i - r) % etp) for i in range(etp)])

    def forward(array, r):
        return lax.ppermute(array, "etp", [(i, (i + r) % etp) for i in range(etp)])

    ahead = (0, 2, 1, 3)
    with jax.named_scope("group_exchange"):
        token_parts = split_columns(tokens, x, [-r for r in ahead])
        group_tokens = jnp.concatenate(
            [token_parts[0]] + [back(token_parts[k], ahead[k]) for k in (1, 2, 3)]
        )
        own_routes = routes.reshape(1, own_rows)
        route_blocks = [own_routes] + [back(own_routes, r) for r in ahead[1:]]
        scales = jnp.exp2(exponents.astype(F32))[:, None]
        hidden_parts = split_columns(hidden_grad, x, [-r for r in ahead], scales)
        group_hidden = jnp.concatenate(
            [hidden_parts[0]] + [back(hidden_parts[k], ahead[k]) for k in (1, 2, 3)]
        )

    with jax.named_scope("slots"):
        select = slot_matrix(route_blocks, x, ahead, experts, capacity)

    def pick(rows):
        return jnp.dot(select, rows, preferred_element_type=F32).astype(BF)

    def to_experts(array):
        return lax.all_to_all(array, "expert", split_axis=0, concat_axis=0, tiled=True)

    with jax.named_scope("send_tokens"):
        packed_tokens = pick(group_tokens).reshape(experts, capacity // 2, 2, quarter)
        packed_hidden = pick(group_hidden).reshape(experts, capacity * hidden // 128, 128)
        arrived, packed_hidden = lax.optimization_barrier((to_experts(packed_tokens), packed_hidden))
        own_block = arrived.reshape(slots, quarter)
    with jax.named_scope("send_hidden"):
        scaled = to_experts(packed_hidden).reshape(slots, hidden)

    half = slots // 2
    with jax.named_scope("gather_width"):
        own_sums = up_sums((own_block,), (0,), gate_w, up_w, x)
        left_block, right_block, *own_sums = lax.optimization_barrier(
            (forward(own_block, 1), back(own_block, 1), *own_sums)
        )
        far_upper, far_lower = forward(left_block[:half], 1), back(right_block[half:], 1)
    with jax.named_scope("pre_activations"):
        gate, up = up_sums((right_block, left_block), (1, 3), gate_w, up_w, x, own_sums)
        for_gate, for_up = up_last(far_upper, far_lower, in_hbm(gate), in_hbm(up), 2, gate_w, up_w, x)
    with jax.named_scope("input_partials"):
        grad_gate, grad_up, far_top, far_bottom = down_first(
            scaled, for_gate, for_up, 2, gate_w, up_w, x
        )
        right_bottom, left_top = down_halves(
            grad_gate, grad_up, gate_w, up_w, x, ((1, 1), (3, 0)), BF
        )
        right_top, left_bottom = down_halves(
            grad_gate, grad_up, gate_w, up_w, x, ((1, 0), (3, 1)), F32
        )
        own_top, own_bottom = down_halves(
            grad_gate, grad_up, gate_w, up_w, x, ((0, 0), (0, 1)), F32
        )
    with jax.named_scope("sum_quarters"):
        passed_top, passed_bottom = forward(far_top, 1), back(far_bottom, 1)
        from_left_bottom, from_right_top = forward(right_bottom, 1), back(left_top, 1)
        from_left_top = forward((right_top + passed_top.astype(F32)).astype(BF), 1)
        from_right_bottom = back((left_bottom + passed_bottom.astype(F32)).astype(BF), 1)
        summed = sum_halves(
            (own_top, from_left_top, from_right_top),
            (own_bottom, from_left_bottom, from_right_bottom),
        )
    with jax.named_scope("return_tokens"):
        returned = to_experts(summed.reshape(experts, capacity // 2, 2, quarter))
        rows = returned.reshape(slots, quarter)
        group_rows = lax.dot_general(
            select, rows, (((0,), (0,)), ((), ())), preferred_element_type=F32
        ).astype(BF)
        parts = [group_rows[k * own_rows : (k + 1) * own_rows] for k in range(4)]
        blocks = [parts[0]] + [forward(parts[k], ahead[k]) for k in (1, 2, 3)]
        return join_columns(blocks, x, [-r for r in ahead])


def solution(mesh):
    placed = (
        P(("expert", "etp"), None),
        P(("expert", "etp"), None),
        P(("expert", "etp"), None),
        P(("expert", "etp")),
        P("expert", None, "etp"),
        P("expert", None, "etp"),
    )
    return jax.shard_map(
        on_device, mesh=mesh, in_specs=placed, out_specs=P(("expert", "etp"), None), check_vma=False
    )
```

```python
import jax
import jax.numpy as jnp
from jax import lax
from jax.experimental import pallas as pl
from jax.experimental.pallas import tpu as pltpu
from jax.sharding import PartitionSpec as P

BF = jnp.bfloat16
F32 = jnp.float32
VMEM_LIMIT = 20 * 1024 * 1024


def cost(flops, nbytes, trans=0):
    return pl.CostEstimate(flops=flops, bytes_accessed=nbytes, transcendentals=trans)


def params(grid_rank=1):
    return pltpu.CompilerParams(
        dimension_semantics=("arbitrary",) * grid_rank, vmem_limit_bytes=VMEM_LIMIT
    )


def in_hbm(array):
    return pltpu.with_memory_space_constraint(array, pltpu.HBM)


def quarter_at(x_ref, ahead):
    return (x_ref[0] + ahead) & 3


def split_columns(array, x, offsets, scale=None):
    rows, columns = array.shape
    width = columns // 4

    def kernel(x_ref, *refs):
        scale_refs = refs[4:-4]
        for source, target in zip(refs[:4], refs[-4:]):
            if scale_refs:
                target[...] = (source[...].astype(F32) * scale_refs[0][...]).astype(BF)
            else:
                target[...] = source[...]

    def block(offset):
        return pl.BlockSpec((rows, width), lambda i, x_ref: (0, quarter_at(x_ref, offset)))

    extra = [] if scale is None else [scale]
    return pl.pallas_call(
        kernel,
        grid_spec=pltpu.PrefetchScalarGridSpec(
            num_scalar_prefetch=1,
            grid=(1,),
            in_specs=[block(offset) for offset in offsets]
            + [pl.BlockSpec((rows, 1), lambda i, x_ref: (0, 0)) for _ in extra],
            out_specs=[pl.BlockSpec((rows, width), lambda i, x_ref: (0, 0))] * 4,
        ),
        out_shape=[jax.ShapeDtypeStruct((rows, width), BF)] * 4,
        compiler_params=params(),
        cost_estimate=cost(rows * columns, 4 * rows * columns),
        name="split_columns",
    )(x, array, array, array, array, *extra)


def join_columns(blocks, x, offsets):
    rows, width = blocks[0].shape

    def kernel(x_ref, b0, b1, b2, b3, out):
        for offset, block in zip(offsets, (b0, b1, b2, b3)):
            start = pl.multiple_of(quarter_at(x_ref, offset) * width, 128)
            out[:, pl.ds(start, width)] = block[...]

    return pl.pallas_call(
        kernel,
        grid_spec=pltpu.PrefetchScalarGridSpec(
            num_scalar_prefetch=1,
            grid=(1,),
            in_specs=[pl.BlockSpec((rows, width), lambda i, x_ref: (0, 0))] * 4,
            out_specs=pl.BlockSpec((rows, 4 * width), lambda i, x_ref: (0, 0)),
        ),
        out_shape=jax.ShapeDtypeStruct((rows, 4 * width), BF),
        compiler_params=params(),
        cost_estimate=cost(0, 16 * rows * width),
        name="join_columns",
    )(x, *blocks)


def slot_index(group_routes, x, offsets, experts, capacity):
    own_rows = group_routes.shape[1]
    group = own_rows * len(offsets)

    def kernel(x_ref, all_routes, out):
        routes = jnp.concatenate(
            [all_routes[pl.ds(quarter_at(x_ref, offset), 1), :] for offset in offsets], axis=1
        )

        def places(axis):
            row = lax.broadcasted_iota(jnp.int32, (group, group), axis)
            block = row // own_rows
            offset = jnp.zeros_like(row)
            for k, value in enumerate(offsets):
                offset = jnp.where(block == k, value, offset)
            return ((x_ref[0] + offset) & 3) * own_rows + row % own_rows

        before = jnp.where(places(0) < places(1), 1.0, 0.0).astype(BF)
        same = lax.broadcasted_iota(jnp.int32, (experts, group), 0) == routes
        named = jnp.where(same, 1.0, 0.0)
        counts = jnp.dot(named.astype(BF), before, preferred_element_type=F32)
        rank = jnp.sum(named * counts, axis=0, keepdims=True).astype(jnp.int32)
        out[...] = routes * capacity + rank

    return pl.pallas_call(
        kernel,
        grid_spec=pltpu.PrefetchScalarGridSpec(
            num_scalar_prefetch=1,
            grid=(1,),
            in_specs=[pl.BlockSpec(group_routes.shape, lambda i, x_ref: (0, 0))],
            out_specs=pl.BlockSpec((1, group), lambda i, x_ref: (0, 0)),
        ),
        out_shape=jax.ShapeDtypeStruct((1, group), jnp.int32),
        compiler_params=params(),
        cost_estimate=cost(0, 0),
        name="slot_index",
    )(x, group_routes)


HIDDEN_TILE = 512
SCHEDULE_WEIGHT = 6


def up_sums(blocks, offsets, gate_weight, up_weight, x, so_far=()):
    rows, depth = blocks[0].shape
    hidden = gate_weight.shape[1]
    count = len(offsets)

    def kernel(x_ref, *refs):
        starts = refs[3 * count : -2]
        for n, out in enumerate(refs[-2:]):
            weights = refs[(1 + n) * count : (2 + n) * count]
            total = jnp.dot(refs[0][...], weights[0][...], preferred_element_type=F32)
            for block, w in zip(refs[1:count], weights[1:]):
                total += jnp.dot(block[...], w[...], preferred_element_type=F32)
            if starts:
                total += starts[n][...]
            out[...] = total

    def weight(offset):
        return pl.BlockSpec((depth, HIDDEN_TILE), lambda j, x_ref: (quarter_at(x_ref, offset), j))

    tiled = pl.BlockSpec((rows, HIDDEN_TILE), lambda j, x_ref: (0, j))
    if so_far:
        out_shape = [pltpu.HBM((rows, hidden), F32)] * 2
    else:
        out_shape = [jax.ShapeDtypeStruct((rows, hidden), F32)] * 2
    return pl.pallas_call(
        kernel,
        grid_spec=pltpu.PrefetchScalarGridSpec(
            num_scalar_prefetch=1,
            grid=(hidden // HIDDEN_TILE,),
            in_specs=[pl.BlockSpec((rows, depth), lambda j, x_ref: (0, 0))] * count
            + [weight(offset) for offset in offsets] * 2
            + [tiled] * len(so_far),
            out_specs=[tiled, tiled],
        ),
        out_shape=out_shape,
        compiler_params=params(),
        cost_estimate=cost(
            SCHEDULE_WEIGHT * 4 * count * rows * depth * hidden, 4 * count * depth * hidden + 16 * rows * hidden
        ),
        name="up_sums",
    )(x, *blocks, *([gate_weight] * count), *([up_weight] * count), *so_far)


CONTRACT_LAST = (((1,), (1,)), ((), ()))


def down_dot(gg, gu, wg, wu):
    total = lax.dot_general(gg, wg, CONTRACT_LAST, preferred_element_type=F32)
    return total + lax.dot_general(gu, wu, CONTRACT_LAST, preferred_element_type=F32)


def up_last(upper, lower, gate, up, offset, gate_weight, up_weight, x):
    half, depth = upper.shape
    rows, hidden = gate.shape

    def kernel(x_ref, top, bottom, g_in, u_in, wg, wu, for_gate, for_up):
        for k, t in enumerate((top, bottom)):
            part = slice(k * half, (k + 1) * half)
            g = g_in[part, :] + jnp.dot(t[...], wg[...], preferred_element_type=F32)
            u = u_in[part, :] + jnp.dot(t[...], wu[...], preferred_element_type=F32)
            s = 1.0 / (1.0 + jnp.exp(-g))
            for_gate[part, :] = u * s * (1.0 + g * (1.0 - s))
            for_up[part, :] = g * s

    weight = pl.BlockSpec((depth, HIDDEN_TILE), lambda j, x_ref: (quarter_at(x_ref, offset), j))
    tiled = pl.BlockSpec((rows, HIDDEN_TILE), lambda j, x_ref: (0, j))
    halves = [pl.BlockSpec((half, depth), lambda j, x_ref: (0, 0))] * 2
    return pl.pallas_call(
        kernel,
        grid_spec=pltpu.PrefetchScalarGridSpec(
            num_scalar_prefetch=1,
            grid=(hidden // HIDDEN_TILE,),
            in_specs=halves + [tiled] * 2 + [weight] * 2,
            out_specs=[tiled] * 2,
        ),
        out_shape=[pltpu.HBM((rows, hidden), F32)] * 2,
        compiler_params=params(),
        cost_estimate=cost(
            4 * rows * depth * hidden, 4 * depth * hidden + 16 * rows * hidden, rows * hidden
        ),
        name="up_last",
    )(x, upper, lower, gate, up, gate_weight, up_weight)


def down_first(scaled, for_gate, for_up, offset, gate_weight, up_weight, x):
    rows, hidden = scaled.shape
    depth = gate_weight.shape[0] // 4
    half = rows // 2
    steps = hidden // HIDDEN_TILE

    def kernel(x_ref, h, a, b, wg, wu, gg_out, gu_out, out_top, out_bottom, total):
        step = pl.program_id(0)
        for k, out in enumerate((out_top, out_bottom)):
            part = slice(k * half, (k + 1) * half)
            h_part = h[part, :].astype(F32)
            gg = (h_part * a[part, :]).astype(BF)
            gu = (h_part * b[part, :]).astype(BF)
            gg_out[part, :] = gg
            gu_out[part, :] = gu
            value = down_dot(gg, gu, wg[...], wu[...])

            @pl.when(step == 0)
            def _():
                total[part, :] = value

            @pl.when((step > 0) & (step < steps - 1))
            def _():
                total[part, :] += value

            @pl.when(step == steps - 1)
            def _():
                out[...] = (total[part, :] + value).astype(BF)

    weight = pl.BlockSpec((depth, HIDDEN_TILE), lambda j, x_ref: (quarter_at(x_ref, offset), j))
    tiled = pl.BlockSpec((rows, HIDDEN_TILE), lambda j, x_ref: (0, j))
    halves = [pl.BlockSpec((half, depth), lambda j, x_ref: (0, 0))] * 2
    return pl.pallas_call(
        kernel,
        grid_spec=pltpu.PrefetchScalarGridSpec(
            num_scalar_prefetch=1,
            grid=(steps,),
            in_specs=[tiled] * 3 + [weight] * 2,
            out_specs=[tiled] * 2 + halves,
            scratch_shapes=[pltpu.VMEM((rows, depth), F32)],
        ),
        out_shape=[jax.ShapeDtypeStruct((rows, hidden), BF)] * 2
        + [jax.ShapeDtypeStruct((half, depth), BF)] * 2,
        compiler_params=params(),
        cost_estimate=cost(4 * rows * depth * hidden, 4 * depth * hidden + 14 * rows * hidden),
        name="down_first",
    )(x, scaled, in_hbm(for_gate), in_hbm(for_up), gate_weight, up_weight)


def down_halves(grad_gate, grad_up, gate_weight, up_weight, x, pieces, dtype):
    rows, hidden = grad_gate.shape
    depth = gate_weight.shape[0] // 4
    half = rows // 2
    count = len(pieces)

    def at_step(j, values):
        chosen = values[0]
        for k in range(1, count):
            chosen = jnp.where(j == k, values[k], chosen)
        return chosen

    def kernel(x_ref, gg, gu, wg, wu, *outs):
        for k in range(count):

            @pl.when(pl.program_id(0) == k)
            def _():
                outs[k][...] = down_dot(gg[...], gu[...], wg[...], wu[...]).astype(dtype)

    weight = pl.BlockSpec(
        (depth, hidden),
        lambda j, x_ref: (quarter_at(x_ref, at_step(j, [offset for offset, _ in pieces])), 0),
    )
    grads = pl.BlockSpec((half, hidden), lambda j, x_ref: (at_step(j, [k for _, k in pieces]), 0))
    return pl.pallas_call(
        kernel,
        grid_spec=pltpu.PrefetchScalarGridSpec(
            num_scalar_prefetch=1,
            grid=(count,),
            in_specs=[grads] * 2 + [weight] * 2,
            out_specs=[pl.BlockSpec((half, depth), lambda j, x_ref: (0, 0))] * count,
        ),
        out_shape=[jax.ShapeDtypeStruct((half, depth), dtype)] * count,
        compiler_params=params(),
        cost_estimate=cost(
            1 * count * half * depth * hidden, 4 * count * depth * hidden + 4 * count * half * hidden
        ),
        name="down_halves",
    )(x, grad_gate, grad_up, gate_weight, up_weight)


def sum_halves(upper, lower):
    rows, width = upper[0].shape
    count = len(upper)

    def kernel(*refs):
        out = refs[-1]
        for k, half in enumerate((refs[:count], refs[count : 2 * count])):
            total = half[0][...].astype(F32)
            for ref in half[1:]:
                total = total + ref[...].astype(F32)
            out[k * rows : (k + 1) * rows, :] = total.astype(BF)

    return pl.pallas_call(
        kernel,
        out_shape=jax.ShapeDtypeStruct((2 * rows, width), BF),
        compiler_params=pltpu.CompilerParams(vmem_limit_bytes=VMEM_LIMIT),
        cost_estimate=cost(4 * rows * width, 16 * rows * width),
        name="sum_halves",
    )(*upper, *lower)


def on_device(tokens, hidden_grad, routes, exponents, gate_weight, up_weight):
    etp = lax.axis_size("etp")
    experts = lax.axis_size("expert")
    own_rows, features = tokens.shape
    capacity = 5 * own_rows * etp // (4 * experts)
    slots = experts * capacity
    quarter, hidden = features // 4, hidden_grad.shape[1] // 4
    x = lax.axis_index("etp").astype(jnp.int32).reshape(1)
    gate_w, up_w = in_hbm(gate_weight[0]), in_hbm(up_weight[0])
    tokens, hidden_grad = in_hbm(tokens), in_hbm(hidden_grad)

    def back(array, r):
        return lax.ppermute(array, "etp", [(i, (i - r) % etp) for i in range(etp)])

    def forward(array, r):
        return lax.ppermute(array, "etp", [(i, (i + r) % etp) for i in range(etp)])

    ahead = (0, 2, 1, 3)
    with jax.named_scope("group_exchange"):
        token_parts = split_columns(tokens, x, [-r for r in ahead])
        group_tokens = jnp.concatenate(
            [token_parts[0]] + [back(token_parts[k], ahead[k]) for k in (1, 2, 3)]
        )
        group_routes = lax.all_gather(routes.reshape(1, own_rows), "etp", axis=0, tiled=True)
        scales = jnp.exp2(exponents.astype(F32))[:, None]
        hidden_parts = split_columns(hidden_grad, x, [-r for r in ahead], scales)
        group_hidden = jnp.concatenate(
            [hidden_parts[0]] + [back(hidden_parts[k], ahead[k]) for k in (1, 2, 3)]
        )

    with jax.named_scope("slots"):
        slot = slot_index(group_routes, x, ahead, experts, capacity)
        select = (jnp.arange(slots, dtype=jnp.int32)[:, None] == slot).astype(BF)

    def pick(rows):
        return jnp.dot(select, rows, preferred_element_type=F32).astype(BF)

    def to_experts(array):
        return lax.all_to_all(array, "expert", split_axis=0, concat_axis=0, tiled=True)

    with jax.named_scope("send_tokens"):
        packed_tokens = pick(group_tokens).reshape(experts, capacity // 2, 2, quarter)
        packed_hidden = pick(group_hidden).reshape(experts, capacity // 2, 2, hidden)
        arrived, packed_hidden = lax.optimization_barrier((to_experts(packed_tokens), packed_hidden))
        own_block = arrived.reshape(slots, quarter)
    with jax.named_scope("send_hidden"):
        scaled = to_experts(packed_hidden).reshape(slots, hidden)

    half = slots // 2
    with jax.named_scope("gather_width"):
        own_sums = up_sums((own_block,), (0,), gate_w, up_w, x)
        left_block, right_block, *own_sums = lax.optimization_barrier(
            (forward(own_block, 1), back(own_block, 1), *own_sums)
        )
        far_upper, far_lower = forward(left_block[:half], 1), back(right_block[half:], 1)
    with jax.named_scope("pre_activations"):
        gate, up = up_sums((right_block, left_block), (1, 3), gate_w, up_w, x, own_sums)
        for_gate, for_up = up_last(far_upper, far_lower, in_hbm(gate), in_hbm(up), 2, gate_w, up_w, x)
    with jax.named_scope("input_partials"):
        grad_gate, grad_up, far_top, far_bottom = down_first(
            scaled, for_gate, for_up, 2, gate_w, up_w, x
        )
        right_bottom, left_top = down_halves(
            grad_gate, grad_up, gate_w, up_w, x, ((1, 1), (3, 0)), BF
        )
        right_top, left_bottom = down_halves(
            grad_gate, grad_up, gate_w, up_w, x, ((1, 0), (3, 1)), F32
        )
        own_top, own_bottom = down_halves(
            grad_gate, grad_up, gate_w, up_w, x, ((0, 0), (0, 1)), F32
        )
    with jax.named_scope("sum_quarters"):
        passed_top, passed_bottom = forward(far_top, 1), back(far_bottom, 1)
        from_left_bottom, from_right_top = forward(right_bottom, 1), back(left_top, 1)
        from_left_top = forward((right_top + passed_top.astype(F32)).astype(BF), 1)
        from_right_bottom = back((left_bottom + passed_bottom.astype(F32)).astype(BF), 1)
        summed = sum_halves(
            (own_top, from_left_top, from_right_top),
            (own_bottom, from_left_bottom, from_right_bottom),
        )
    with jax.named_scope("return_tokens"):
        returned = to_experts(summed.reshape(experts, capacity // 2, 2, quarter))
        rows = returned.reshape(slots, quarter)
        group_rows = lax.dot_general(
            select, rows, (((0,), (0,)), ((), ())), preferred_element_type=F32
        ).astype(BF)
        parts = [group_rows[k * own_rows : (k + 1) * own_rows] for k in range(4)]
        blocks = [parts[0]] + [forward(parts[k], ahead[k]) for k in (1, 2, 3)]
        return join_columns(blocks, x, [-r for r in ahead])


def solution(mesh):
    placed = (
        P(("expert", "etp"), None),
        P(("expert", "etp"), None),
        P(("expert", "etp"), None),
        P(("expert", "etp")),
        P("expert", None, "etp"),
        P("expert", None, "etp"),
    )
    return jax.shard_map(
        on_device, mesh=mesh, in_specs=placed, out_specs=P(("expert", "etp"), None), check_vma=False
    )
```

```python
import jax
import jax.numpy as jnp
from jax import lax
from jax.experimental import pallas as pl
from jax.experimental.pallas import tpu as pltpu
from jax.sharding import PartitionSpec as P

BF = jnp.bfloat16
F32 = jnp.float32
VMEM_LIMIT = 20 * 1024 * 1024


def cost(flops, nbytes, trans=0):
    return pl.CostEstimate(flops=flops, bytes_accessed=nbytes, transcendentals=trans)


def params(grid_rank=1):
    return pltpu.CompilerParams(
        dimension_semantics=("arbitrary",) * grid_rank, vmem_limit_bytes=VMEM_LIMIT
    )


def in_hbm(array):
    return pltpu.with_memory_space_constraint(array, pltpu.HBM)


def quarter_at(x_ref, ahead):
    return (x_ref[0] + ahead) & 3


def split_columns(array, x, offsets, scale=None):
    rows, columns = array.shape
    width = columns // 4

    def kernel(x_ref, *refs):
        scale_refs = refs[4:-4]
        for source, target in zip(refs[:4], refs[-4:]):
            if scale_refs:
                target[...] = (source[...].astype(F32) * scale_refs[0][...]).astype(BF)
            else:
                target[...] = source[...]

    def block(offset):
        return pl.BlockSpec((rows, width), lambda i, x_ref: (0, quarter_at(x_ref, offset)))

    extra = [] if scale is None else [scale]
    return pl.pallas_call(
        kernel,
        grid_spec=pltpu.PrefetchScalarGridSpec(
            num_scalar_prefetch=1,
            grid=(1,),
            in_specs=[block(offset) for offset in offsets]
            + [pl.BlockSpec((rows, 1), lambda i, x_ref: (0, 0)) for _ in extra],
            out_specs=[pl.BlockSpec((rows, width), lambda i, x_ref: (0, 0))] * 4,
        ),
        out_shape=[jax.ShapeDtypeStruct((rows, width), BF)] * 4,
        compiler_params=params(),
        cost_estimate=cost(rows * columns, 4 * rows * columns),
        name="split_columns",
    )(x, array, array, array, array, *extra)


def join_columns(blocks, x, offsets):
    rows, width = blocks[0].shape

    def kernel(x_ref, b0, b1, b2, b3, out):
        for offset, block in zip(offsets, (b0, b1, b2, b3)):
            start = pl.multiple_of(quarter_at(x_ref, offset) * width, 128)
            out[:, pl.ds(start, width)] = block[...]

    return pl.pallas_call(
        kernel,
        grid_spec=pltpu.PrefetchScalarGridSpec(
            num_scalar_prefetch=1,
            grid=(1,),
            in_specs=[pl.BlockSpec((rows, width), lambda i, x_ref: (0, 0))] * 4,
            out_specs=pl.BlockSpec((rows, 4 * width), lambda i, x_ref: (0, 0)),
        ),
        out_shape=jax.ShapeDtypeStruct((rows, 4 * width), BF),
        compiler_params=params(),
        cost_estimate=cost(0, 16 * rows * width),
        name="join_columns",
    )(x, *blocks)


def slot_index(group_routes, x, offsets, experts, capacity):
    own_rows = group_routes.shape[1]
    group = own_rows * len(offsets)

    def kernel(x_ref, all_routes, out):
        routes = jnp.concatenate(
            [all_routes[pl.ds(quarter_at(x_ref, offset), 1), :] for offset in offsets], axis=1
        )

        def places(axis):
            row = lax.broadcasted_iota(jnp.int32, (group, group), axis)
            block = row // own_rows
            offset = jnp.zeros_like(row)
            for k, value in enumerate(offsets):
                offset = jnp.where(block == k, value, offset)
            return ((x_ref[0] + offset) & 3) * own_rows + row % own_rows

        before = jnp.where(places(0) < places(1), 1.0, 0.0).astype(BF)
        same = lax.broadcasted_iota(jnp.int32, (experts, group), 0) == routes
        named = jnp.where(same, 1.0, 0.0)
        counts = jnp.dot(named.astype(BF), before, preferred_element_type=F32)
        rank = jnp.sum(named * counts, axis=0, keepdims=True).astype(jnp.int32)
        out[...] = routes * capacity + rank

    return pl.pallas_call(
        kernel,
        grid_spec=pltpu.PrefetchScalarGridSpec(
            num_scalar_prefetch=1,
            grid=(1,),
            in_specs=[pl.BlockSpec(group_routes.shape, lambda i, x_ref: (0, 0))],
            out_specs=pl.BlockSpec((1, group), lambda i, x_ref: (0, 0)),
        ),
        out_shape=jax.ShapeDtypeStruct((1, group), jnp.int32),
        compiler_params=params(),
        cost_estimate=cost(0, 0),
        name="slot_index",
    )(x, group_routes)


HIDDEN_TILE = 512
SCHEDULE_WEIGHT = 6


def up_sums(blocks, offsets, gate_weight, up_weight, x, so_far=()):
    rows, depth = blocks[0].shape
    hidden = gate_weight.shape[1]
    count = len(offsets)

    def kernel(x_ref, *refs):
        starts = refs[3 * count : -2]
        for n, out in enumerate(refs[-2:]):
            weights = refs[(1 + n) * count : (2 + n) * count]
            total = jnp.dot(refs[0][...], weights[0][...], preferred_element_type=F32)
            for block, w in zip(refs[1:count], weights[1:]):
                total += jnp.dot(block[...], w[...], preferred_element_type=F32)
            if starts:
                total += starts[n][...]
            out[...] = total

    def weight(offset):
        return pl.BlockSpec((depth, HIDDEN_TILE), lambda j, x_ref: (quarter_at(x_ref, offset), j))

    tiled = pl.BlockSpec((rows, HIDDEN_TILE), lambda j, x_ref: (0, j))
    if so_far:
        out_shape = [pltpu.HBM((rows, hidden), F32)] * 2
    else:
        out_shape = [jax.ShapeDtypeStruct((rows, hidden), F32)] * 2
    return pl.pallas_call(
        kernel,
        grid_spec=pltpu.PrefetchScalarGridSpec(
            num_scalar_prefetch=1,
            grid=(hidden // HIDDEN_TILE,),
            in_specs=[pl.BlockSpec((rows, depth), lambda j, x_ref: (0, 0))] * count
            + [weight(offset) for offset in offsets] * 2
            + [tiled] * len(so_far),
            out_specs=[tiled, tiled],
        ),
        out_shape=out_shape,
        compiler_params=params(),
        cost_estimate=cost(
            SCHEDULE_WEIGHT * 4 * count * rows * depth * hidden, 4 * count * depth * hidden + 16 * rows * hidden
        ),
        name="up_sums",
    )(x, *blocks, *([gate_weight] * count), *([up_weight] * count), *so_far)


CONTRACT_LAST = (((1,), (1,)), ((), ()))


def down_dot(gg, gu, wg, wu):
    total = lax.dot_general(gg, wg, CONTRACT_LAST, preferred_element_type=F32)
    return total + lax.dot_general(gu, wu, CONTRACT_LAST, preferred_element_type=F32)


def up_last(upper, lower, gate, up, offset, gate_weight, up_weight, x):
    half, depth = upper.shape
    rows, hidden = gate.shape

    def kernel(x_ref, top, bottom, g_in, u_in, wg, wu, for_gate, for_up):
        for k, t in enumerate((top, bottom)):
            part = slice(k * half, (k + 1) * half)
            g = g_in[part, :] + jnp.dot(t[...], wg[...], preferred_element_type=F32)
            u = u_in[part, :] + jnp.dot(t[...], wu[...], preferred_element_type=F32)
            s = 1.0 / (1.0 + jnp.exp(-g))
            for_gate[part, :] = u * s * (1.0 + g * (1.0 - s))
            for_up[part, :] = g * s

    weight = pl.BlockSpec((depth, HIDDEN_TILE), lambda j, x_ref: (quarter_at(x_ref, offset), j))
    tiled = pl.BlockSpec((rows, HIDDEN_TILE), lambda j, x_ref: (0, j))
    halves = [pl.BlockSpec((half, depth), lambda j, x_ref: (0, 0))] * 2
    return pl.pallas_call(
        kernel,
        grid_spec=pltpu.PrefetchScalarGridSpec(
            num_scalar_prefetch=1,
            grid=(hidden // HIDDEN_TILE,),
            in_specs=halves + [tiled] * 2 + [weight] * 2,
            out_specs=[tiled] * 2,
        ),
        out_shape=[pltpu.HBM((rows, hidden), F32)] * 2,
        compiler_params=params(),
        cost_estimate=cost(
            4 * rows * depth * hidden, 4 * depth * hidden + 16 * rows * hidden, rows * hidden
        ),
        name="up_last",
    )(x, upper, lower, gate, up, gate_weight, up_weight)


def down_first(scaled, for_gate, for_up, offset, gate_weight, up_weight, x):
    rows, hidden = scaled.shape
    depth = gate_weight.shape[0] // 4
    half = rows // 2
    steps = hidden // HIDDEN_TILE

    def kernel(x_ref, h, a, b, wg, wu, gg_out, gu_out, out_top, out_bottom, total):
        step = pl.program_id(0)
        for k, out in enumerate((out_top, out_bottom)):
            part = slice(k * half, (k + 1) * half)
            h_part = h[part, :].astype(F32)
            gg = (h_part * a[part, :]).astype(BF)
            gu = (h_part * b[part, :]).astype(BF)
            gg_out[part, :] = gg
            gu_out[part, :] = gu
            value = down_dot(gg, gu, wg[...], wu[...])

            @pl.when(step == 0)
            def _():
                total[part, :] = value

            @pl.when((step > 0) & (step < steps - 1))
            def _():
                total[part, :] += value

            @pl.when(step == steps - 1)
            def _():
                out[...] = (total[part, :] + value).astype(BF)

    weight = pl.BlockSpec((depth, HIDDEN_TILE), lambda j, x_ref: (quarter_at(x_ref, offset), j))
    tiled = pl.BlockSpec((rows, HIDDEN_TILE), lambda j, x_ref: (0, j))
    halves = [pl.BlockSpec((half, depth), lambda j, x_ref: (0, 0))] * 2
    return pl.pallas_call(
        kernel,
        grid_spec=pltpu.PrefetchScalarGridSpec(
            num_scalar_prefetch=1,
            grid=(steps,),
            in_specs=[tiled] * 3 + [weight] * 2,
            out_specs=[tiled] * 2 + halves,
            scratch_shapes=[pltpu.VMEM((rows, depth), F32)],
        ),
        out_shape=[jax.ShapeDtypeStruct((rows, hidden), BF)] * 2
        + [jax.ShapeDtypeStruct((half, depth), BF)] * 2,
        compiler_params=params(),
        cost_estimate=cost(4 * rows * depth * hidden, 4 * depth * hidden + 14 * rows * hidden),
        name="down_first",
    )(x, scaled, in_hbm(for_gate), in_hbm(for_up), gate_weight, up_weight)


def down_halves(grad_gate, grad_up, gate_weight, up_weight, x, pieces, dtype):
    rows, hidden = grad_gate.shape
    depth = gate_weight.shape[0] // 4
    half = rows // 2
    count = len(pieces)

    def at_step(j, values):
        chosen = values[0]
        for k in range(1, count):
            chosen = jnp.where(j == k, values[k], chosen)
        return chosen

    def kernel(x_ref, gg, gu, wg, wu, *outs):
        for k in range(count):

            @pl.when(pl.program_id(0) == k)
            def _():
                outs[k][...] = down_dot(gg[...], gu[...], wg[...], wu[...]).astype(dtype)

    weight = pl.BlockSpec(
        (depth, hidden),
        lambda j, x_ref: (quarter_at(x_ref, at_step(j, [offset for offset, _ in pieces])), 0),
    )
    grads = pl.BlockSpec((half, hidden), lambda j, x_ref: (at_step(j, [k for _, k in pieces]), 0))
    return pl.pallas_call(
        kernel,
        grid_spec=pltpu.PrefetchScalarGridSpec(
            num_scalar_prefetch=1,
            grid=(count,),
            in_specs=[grads] * 2 + [weight] * 2,
            out_specs=[pl.BlockSpec((half, depth), lambda j, x_ref: (0, 0))] * count,
        ),
        out_shape=[jax.ShapeDtypeStruct((half, depth), dtype)] * count,
        compiler_params=params(),
        cost_estimate=cost(
            1 * count * half * depth * hidden, 4 * count * depth * hidden + 4 * count * half * hidden
        ),
        name="down_halves",
    )(x, grad_gate, grad_up, gate_weight, up_weight)


def sum_halves(upper, lower):
    rows, width = upper[0].shape
    count = len(upper)

    def kernel(*refs):
        out = refs[-1]
        for k, half in enumerate((refs[:count], refs[count : 2 * count])):
            total = half[0][...].astype(F32)
            for ref in half[1:]:
                total = total + ref[...].astype(F32)
            out[k * rows : (k + 1) * rows, :] = total.astype(BF)

    return pl.pallas_call(
        kernel,
        out_shape=jax.ShapeDtypeStruct((2 * rows, width), BF),
        compiler_params=pltpu.CompilerParams(vmem_limit_bytes=VMEM_LIMIT),
        cost_estimate=cost(4 * rows * width, 16 * rows * width),
        name="sum_halves",
    )(*upper, *lower)


def on_device(tokens, hidden_grad, routes, exponents, gate_weight, up_weight):
    etp = lax.axis_size("etp")
    experts = lax.axis_size("expert")
    own_rows, features = tokens.shape
    capacity = 5 * own_rows * etp // (4 * experts)
    slots = experts * capacity
    quarter, hidden = features // 4, hidden_grad.shape[1] // 4
    x = lax.axis_index("etp").astype(jnp.int32).reshape(1)
    gate_w, up_w = in_hbm(gate_weight[0]), in_hbm(up_weight[0])
    tokens, hidden_grad = in_hbm(tokens), in_hbm(hidden_grad)

    def back(array, r):
        return lax.ppermute(array, "etp", [(i, (i - r) % etp) for i in range(etp)])

    def forward(array, r):
        return lax.ppermute(array, "etp", [(i, (i + r) % etp) for i in range(etp)])

    ahead = (0, 2, 1, 3)
    with jax.named_scope("group_exchange"):
        token_parts = split_columns(tokens, x, [-r for r in ahead])
        group_tokens = jnp.concatenate(
            [token_parts[0]] + [back(token_parts[k], ahead[k]) for k in (1, 2, 3)]
        )
        group_routes = lax.all_gather(routes.reshape(1, own_rows), "etp", axis=0, tiled=True)
        scales = jnp.exp2(exponents.astype(F32))[:, None]
        hidden_parts = split_columns(hidden_grad, x, [-r for r in ahead], scales)
        group_hidden = jnp.concatenate(
            [hidden_parts[0]] + [back(hidden_parts[k], ahead[k]) for k in (1, 2, 3)]
        )

    with jax.named_scope("slots"):
        slot = slot_index(group_routes, x, ahead, experts, capacity)
        select = (jnp.arange(slots, dtype=jnp.int32)[:, None] == slot).astype(BF)

    def pick(rows):
        return jnp.dot(select, rows, preferred_element_type=F32).astype(BF)

    def to_experts(array):
        return lax.all_to_all(array, "expert", split_axis=0, concat_axis=0, tiled=True)

    with jax.named_scope("send_tokens"):
        packed_tokens = pick(group_tokens).reshape(experts, capacity // 2, 2, quarter)
        packed_hidden = pick(group_hidden).reshape(experts, capacity * hidden // 128, 128)
        arrived, packed_hidden = lax.optimization_barrier((to_experts(packed_tokens), packed_hidden))
        own_block = arrived.reshape(slots, quarter)
    with jax.named_scope("send_hidden"):
        scaled = to_experts(packed_hidden).reshape(slots, hidden)

    half = slots // 2
    with jax.named_scope("gather_width"):
        own_sums = up_sums((in_hbm(own_block),), (0,), gate_w, up_w, x)
        left_block, right_block, *own_sums = lax.optimization_barrier(
            (forward(own_block, 1), back(own_block, 1), *own_sums)
        )
        far_upper, far_lower = forward(left_block[:half], 1), back(right_block[half:], 1)
    with jax.named_scope("pre_activations"):
        gate, up = up_sums((right_block, left_block), (1, 3), gate_w, up_w, x, own_sums)
        for_gate, for_up = up_last(far_upper, far_lower, in_hbm(gate), in_hbm(up), 2, gate_w, up_w, x)
    with jax.named_scope("input_partials"):
        grad_gate, grad_up, far_top, far_bottom = down_first(
            scaled, for_gate, for_up, 2, gate_w, up_w, x
        )
        right_bottom, left_top = down_halves(
            grad_gate, grad_up, gate_w, up_w, x, ((1, 1), (3, 0)), BF
        )
        right_top, left_bottom = down_halves(
            grad_gate, grad_up, gate_w, up_w, x, ((1, 0), (3, 1)), F32
        )
        own_top, own_bottom = down_halves(
            grad_gate, grad_up, gate_w, up_w, x, ((0, 0), (0, 1)), F32
        )
    with jax.named_scope("sum_quarters"):
        passed_top, passed_bottom = forward(far_top, 1), back(far_bottom, 1)
        from_left_bottom, from_right_top = forward(right_bottom, 1), back(left_top, 1)
        from_left_top = forward((right_top + passed_top.astype(F32)).astype(BF), 1)
        from_right_bottom = back((left_bottom + passed_bottom.astype(F32)).astype(BF), 1)
        summed = sum_halves(
            (own_top, from_left_top, from_right_top),
            (own_bottom, from_left_bottom, from_right_bottom),
        )
    with jax.named_scope("return_tokens"):
        returned = to_experts(summed.reshape(experts, capacity // 2, 2, quarter))
        rows = returned.reshape(slots, quarter)
        group_rows = lax.dot_general(
            select, rows, (((0,), (0,)), ((), ())), preferred_element_type=F32
        ).astype(BF)
        parts = [group_rows[k * own_rows : (k + 1) * own_rows] for k in range(4)]
        blocks = [parts[0]] + [forward(parts[k], ahead[k]) for k in (1, 2, 3)]
        return join_columns(blocks, x, [-r for r in ahead])


def solution(mesh):
    placed = (
        P(("expert", "etp"), None),
        P(("expert", "etp"), None),
        P(("expert", "etp"), None),
        P(("expert", "etp")),
        P("expert", None, "etp"),
        P("expert", None, "etp"),
    )
    return jax.shard_map(
        on_device, mesh=mesh, in_specs=placed, out_specs=P(("expert", "etp"), None), check_vma=False
    )
```

```python
import jax
import jax.numpy as jnp
from jax import lax
from jax.experimental import pallas as pl
from jax.experimental.pallas import tpu as pltpu
from jax.sharding import PartitionSpec as P

BF = jnp.bfloat16
F32 = jnp.float32


def cost(flops, nbytes, trans=0):
    return pl.CostEstimate(flops=flops, bytes_accessed=nbytes, transcendentals=trans)


def params(megabytes=20):
    return pltpu.CompilerParams(
        dimension_semantics=("arbitrary",), vmem_limit_bytes=megabytes * 1024 * 1024
    )


def in_hbm(array):
    return pltpu.with_memory_space_constraint(array, pltpu.HBM)


def quarter_at(x_ref, ahead):
    return (x_ref[0] + ahead) & 3


def split_columns(array, x, offsets, scale=None):
    rows, columns = array.shape
    width = columns // 4

    def kernel(x_ref, *refs):
        scale_refs = refs[4:-4]
        for source, target in zip(refs[:4], refs[-4:]):
            if scale_refs:
                target[...] = (source[...].astype(F32) * scale_refs[0][...]).astype(BF)
            else:
                target[...] = source[...]

    def block(offset):
        return pl.BlockSpec((rows, width), lambda i, x_ref: (0, quarter_at(x_ref, offset)))

    extra = [] if scale is None else [scale]
    return pl.pallas_call(
        kernel,
        grid_spec=pltpu.PrefetchScalarGridSpec(
            num_scalar_prefetch=1,
            grid=(1,),
            in_specs=[block(offset) for offset in offsets]
            + [pl.BlockSpec((rows, 1), lambda i, x_ref: (0, 0)) for _ in extra],
            out_specs=[pl.BlockSpec((rows, width), lambda i, x_ref: (0, 0))] * 4,
        ),
        out_shape=[jax.ShapeDtypeStruct((rows, width), BF)] * 4,
        compiler_params=params(),
        cost_estimate=cost(rows * columns, 4 * rows * columns),
        name="split_columns",
    )(x, array, array, array, array, *extra)


def join_columns(blocks, x, offsets):
    rows, width = blocks[0].shape

    def kernel(x_ref, b0, b1, b2, b3, out):
        for offset, block in zip(offsets, (b0, b1, b2, b3)):
            start = pl.multiple_of(quarter_at(x_ref, offset) * width, 128)
            out[:, pl.ds(start, width)] = block[...]

    return pl.pallas_call(
        kernel,
        grid_spec=pltpu.PrefetchScalarGridSpec(
            num_scalar_prefetch=1,
            grid=(1,),
            in_specs=[pl.BlockSpec((rows, width), lambda i, x_ref: (0, 0))] * 4,
            out_specs=pl.BlockSpec((rows, 4 * width), lambda i, x_ref: (0, 0)),
        ),
        out_shape=jax.ShapeDtypeStruct((rows, 4 * width), BF),
        compiler_params=params(),
        cost_estimate=cost(0, 16 * rows * width),
        name="join_columns",
    )(x, *blocks)


def slot_index(group_routes, x, offsets, experts, capacity):
    own_rows = group_routes.shape[1]
    group = own_rows * len(offsets)

    def kernel(x_ref, all_routes, out):
        routes = jnp.concatenate(
            [all_routes[pl.ds(quarter_at(x_ref, offset), 1), :] for offset in offsets], axis=1
        )

        def places(axis):
            row = lax.broadcasted_iota(jnp.int32, (group, group), axis)
            block = row // own_rows
            offset = jnp.zeros_like(row)
            for k, value in enumerate(offsets):
                offset = jnp.where(block == k, value, offset)
            return ((x_ref[0] + offset) & 3) * own_rows + row % own_rows

        before = jnp.where(places(0) < places(1), 1.0, 0.0).astype(BF)
        same = lax.broadcasted_iota(jnp.int32, (experts, group), 0) == routes
        named = jnp.where(same, 1.0, 0.0)
        counts = jnp.dot(named.astype(BF), before, preferred_element_type=F32)
        rank = jnp.sum(named * counts, axis=0, keepdims=True).astype(jnp.int32)
        out[...] = routes * capacity + rank

    return pl.pallas_call(
        kernel,
        grid_spec=pltpu.PrefetchScalarGridSpec(
            num_scalar_prefetch=1,
            grid=(1,),
            in_specs=[pl.BlockSpec(group_routes.shape, lambda i, x_ref: (0, 0))],
            out_specs=pl.BlockSpec((1, group), lambda i, x_ref: (0, 0)),
        ),
        out_shape=jax.ShapeDtypeStruct((1, group), jnp.int32),
        compiler_params=params(),
        cost_estimate=cost(0, 0),
        name="slot_index",
    )(x, group_routes)


HIDDEN_TILE = 512
SCHEDULE_WEIGHT = 6


def up_sums(blocks, offsets, gate_weight, up_weight, x, so_far=()):
    rows, depth = blocks[0].shape
    hidden = gate_weight.shape[1]
    count = len(offsets)

    def kernel(x_ref, *refs):
        starts = refs[3 * count : -2]
        for n, out in enumerate(refs[-2:]):
            weights = refs[(1 + n) * count : (2 + n) * count]
            total = jnp.dot(refs[0][...], weights[0][...], preferred_element_type=F32)
            for block, w in zip(refs[1:count], weights[1:]):
                total += jnp.dot(block[...], w[...], preferred_element_type=F32)
            if starts:
                total += starts[n][...]
            out[...] = total

    def weight(offset):
        return pl.BlockSpec((depth, HIDDEN_TILE), lambda j, x_ref: (quarter_at(x_ref, offset), j))

    tiled = pl.BlockSpec((rows, HIDDEN_TILE), lambda j, x_ref: (0, j))
    if so_far:
        out_shape = [pltpu.HBM((rows, hidden), F32)] * 2
    else:
        out_shape = [jax.ShapeDtypeStruct((rows, hidden), F32)] * 2
    return pl.pallas_call(
        kernel,
        grid_spec=pltpu.PrefetchScalarGridSpec(
            num_scalar_prefetch=1,
            grid=(hidden // HIDDEN_TILE,),
            in_specs=[pl.BlockSpec((rows, depth), lambda j, x_ref: (0, 0))] * count
            + [weight(offset) for offset in offsets] * 2
            + [tiled] * len(so_far),
            out_specs=[tiled, tiled],
        ),
        out_shape=out_shape,
        compiler_params=params(),
        cost_estimate=cost(
            SCHEDULE_WEIGHT * 4 * count * rows * depth * hidden, 4 * count * depth * hidden + 16 * rows * hidden
        ),
        name="up_sums",
    )(x, *blocks, *([gate_weight] * count), *([up_weight] * count), *so_far)


CONTRACT_LAST = (((1,), (1,)), ((), ()))


def down_dot(gg, gu, wg, wu):
    total = lax.dot_general(gg, wg, CONTRACT_LAST, preferred_element_type=F32)
    return total + lax.dot_general(gu, wu, CONTRACT_LAST, preferred_element_type=F32)


def up_last(upper, lower, gate, up, offset, gate_weight, up_weight, x):
    half, depth = upper.shape
    rows, hidden = gate.shape

    def kernel(x_ref, top, bottom, g_in, u_in, wg, wu, for_gate, for_up):
        for k, t in enumerate((top, bottom)):
            part = slice(k * half, (k + 1) * half)
            g = g_in[part, :] + jnp.dot(t[...], wg[...], preferred_element_type=F32)
            u = u_in[part, :] + jnp.dot(t[...], wu[...], preferred_element_type=F32)
            s = 1.0 / (1.0 + jnp.exp(-g))
            for_gate[part, :] = (u * s * (1.0 + g * (1.0 - s))).astype(BF)
            for_up[part, :] = (g * s).astype(BF)

    weight = pl.BlockSpec((depth, HIDDEN_TILE), lambda j, x_ref: (quarter_at(x_ref, offset), j))
    tiled = pl.BlockSpec((rows, HIDDEN_TILE), lambda j, x_ref: (0, j))
    halves = [pl.BlockSpec((half, depth), lambda j, x_ref: (0, 0))] * 2
    return pl.pallas_call(
        kernel,
        grid_spec=pltpu.PrefetchScalarGridSpec(
            num_scalar_prefetch=1,
            grid=(hidden // HIDDEN_TILE,),
            in_specs=halves + [tiled] * 2 + [weight] * 2,
            out_specs=[tiled] * 2,
        ),
        out_shape=[pltpu.HBM((rows, hidden), BF)] * 2,
        compiler_params=params(),
        cost_estimate=cost(
            4 * rows * depth * hidden, 4 * depth * hidden + 12 * rows * hidden, rows * hidden
        ),
        name="up_last",
    )(x, upper, lower, gate, up, gate_weight, up_weight)


def down_first(scaled, for_gate, for_up, offset, gate_weight, up_weight, x):
    rows, hidden = scaled.shape
    depth = gate_weight.shape[0] // 4
    half = rows // 2

    def kernel(x_ref, h, a, b, wg, wu, gg_out, gu_out, out_top, out_bottom):
        for k, out in enumerate((out_top, out_bottom)):
            part = slice(k * half, (k + 1) * half)
            h_part = h[part, :].astype(F32)
            gg = (h_part * a[part, :].astype(F32)).astype(BF)
            gu = (h_part * b[part, :].astype(F32)).astype(BF)
            gg_out[part, :] = gg
            gu_out[part, :] = gu
            out[...] = down_dot(gg, gu, wg[...], wu[...]).astype(BF)

    weight = pl.BlockSpec((depth, hidden), lambda k, x_ref: (quarter_at(x_ref, offset), 0))
    whole = pl.BlockSpec((rows, hidden), lambda k, x_ref: (0, 0))
    halves = [pl.BlockSpec((half, depth), lambda k, x_ref: (0, 0))] * 2
    return pl.pallas_call(
        kernel,
        grid_spec=pltpu.PrefetchScalarGridSpec(
            num_scalar_prefetch=1,
            grid=(1,),
            in_specs=[whole] * 3 + [weight] * 2,
            out_specs=[whole] * 2 + halves,
        ),
        out_shape=[jax.ShapeDtypeStruct((rows, hidden), BF)] * 2
        + [jax.ShapeDtypeStruct((half, depth), BF)] * 2,
        compiler_params=params(megabytes=30),
        cost_estimate=cost(4 * rows * depth * hidden, 4 * depth * hidden + 10 * rows * hidden),
        name="down_first",
    )(x, scaled, in_hbm(for_gate), in_hbm(for_up), gate_weight, up_weight)


def down_halves(grad_gate, grad_up, gate_weight, up_weight, x, pieces, dtype):
    rows, hidden = grad_gate.shape
    depth = gate_weight.shape[0] // 4
    half = rows // 2
    count = len(pieces)

    def at_step(j, values):
        chosen = values[0]
        for k in range(1, count):
            chosen = jnp.where(j == k, values[k], chosen)
        return chosen

    def kernel(x_ref, gg, gu, wg, wu, *outs):
        for k in range(count):

            @pl.when(pl.program_id(0) == k)
            def _():
                outs[k][...] = down_dot(gg[...], gu[...], wg[...], wu[...]).astype(dtype)

    weight = pl.BlockSpec(
        (depth, hidden),
        lambda j, x_ref: (quarter_at(x_ref, at_step(j, [offset for offset, _ in pieces])), 0),
    )
    grads = pl.BlockSpec((half, hidden), lambda j, x_ref: (at_step(j, [k for _, k in pieces]), 0))
    return pl.pallas_call(
        kernel,
        grid_spec=pltpu.PrefetchScalarGridSpec(
            num_scalar_prefetch=1,
            grid=(count,),
            in_specs=[grads] * 2 + [weight] * 2,
            out_specs=[pl.BlockSpec((half, depth), lambda j, x_ref: (0, 0))] * count,
        ),
        out_shape=[jax.ShapeDtypeStruct((half, depth), dtype)] * count,
        compiler_params=params(),
        cost_estimate=cost(
            1 * count * half * depth * hidden, 4 * count * depth * hidden + 4 * count * half * hidden
        ),
        name="down_halves",
    )(x, grad_gate, grad_up, gate_weight, up_weight)


def sum_halves(upper, lower):
    rows, width = upper[0].shape
    count = len(upper)

    def kernel(*refs):
        out = refs[-1]
        for k, half in enumerate((refs[:count], refs[count : 2 * count])):
            total = half[0][...].astype(F32)
            for ref in half[1:]:
                total = total + ref[...].astype(F32)
            out[k * rows : (k + 1) * rows, :] = total.astype(BF)

    return pl.pallas_call(
        kernel,
        out_shape=jax.ShapeDtypeStruct((2 * rows, width), BF),
        compiler_params=pltpu.CompilerParams(vmem_limit_bytes=20 * 1024 * 1024),
        cost_estimate=cost(4 * rows * width, 16 * rows * width),
        name="sum_halves",
    )(*upper, *lower)


def on_device(tokens, hidden_grad, routes, exponents, gate_weight, up_weight):
    etp = lax.axis_size("etp")
    experts = lax.axis_size("expert")
    own_rows, features = tokens.shape
    capacity = 5 * own_rows * etp // (4 * experts)
    slots = experts * capacity
    quarter, hidden = features // 4, hidden_grad.shape[1] // 4
    x = lax.axis_index("etp").astype(jnp.int32).reshape(1)
    gate_w, up_w = in_hbm(gate_weight[0]), in_hbm(up_weight[0])
    tokens, hidden_grad = in_hbm(tokens), in_hbm(hidden_grad)

    def back(array, r):
        return lax.ppermute(array, "etp", [(i, (i - r) % etp) for i in range(etp)])

    def forward(array, r):
        return lax.ppermute(array, "etp", [(i, (i + r) % etp) for i in range(etp)])

    ahead = (0, 2, 1, 3)
    with jax.named_scope("group_exchange"):
        token_parts = split_columns(tokens, x, [-r for r in ahead])
        group_tokens = jnp.concatenate(
            [token_parts[0]] + [back(token_parts[k], ahead[k]) for k in (1, 2, 3)]
        )
        group_routes = lax.all_gather(routes.reshape(1, own_rows), "etp", axis=0, tiled=True)
        scales = jnp.exp2(exponents.astype(F32))[:, None]
        hidden_parts = split_columns(hidden_grad, x, [-r for r in ahead], scales)
        group_hidden = jnp.concatenate(
            [hidden_parts[0]] + [back(hidden_parts[k], ahead[k]) for k in (1, 2, 3)]
        )

    with jax.named_scope("slots"):
        slot = slot_index(group_routes, x, ahead, experts, capacity)
        select = (jnp.arange(slots, dtype=jnp.int32)[:, None] == slot).astype(BF)

    def pick(rows):
        return jnp.dot(select, rows, preferred_element_type=F32).astype(BF)

    def to_experts(array):
        return lax.all_to_all(array, "expert", split_axis=0, concat_axis=0, tiled=True)

    with jax.named_scope("send_tokens"):
        packed_tokens = pick(group_tokens).reshape(experts, capacity // 2, 2, quarter)
        packed_hidden = pick(group_hidden).reshape(experts, capacity * hidden // 128, 128)
        arrived, packed_hidden = lax.optimization_barrier((to_experts(packed_tokens), packed_hidden))
        own_block = arrived.reshape(slots, quarter)
    with jax.named_scope("send_hidden"):
        scaled = to_experts(packed_hidden).reshape(slots, hidden)

    half = slots // 2
    with jax.named_scope("gather_width"):
        own_sums = up_sums((own_block,), (0,), gate_w, up_w, x)
        left_block, right_block, *own_sums = lax.optimization_barrier(
            (forward(own_block, 1), back(own_block, 1), *own_sums)
        )
        far_upper, far_lower = forward(left_block[:half], 1), back(right_block[half:], 1)
    with jax.named_scope("pre_activations"):
        gate, up = up_sums((in_hbm(right_block), in_hbm(left_block)), (1, 3), gate_w, up_w, x, own_sums)
        for_gate, for_up = up_last(far_upper, far_lower, in_hbm(gate), in_hbm(up), 2, gate_w, up_w, x)
    with jax.named_scope("input_partials"):
        grad_gate, grad_up, far_top, far_bottom = down_first(
            scaled, for_gate, for_up, 2, gate_w, up_w, x
        )
        right_bottom, left_top = down_halves(
            grad_gate, grad_up, gate_w, up_w, x, ((1, 1), (3, 0)), BF
        )
        right_top, left_bottom = down_halves(
            grad_gate, grad_up, gate_w, up_w, x, ((1, 0), (3, 1)), F32
        )
        own_top, own_bottom = down_halves(
            grad_gate, grad_up, gate_w, up_w, x, ((0, 0), (0, 1)), F32
        )
    with jax.named_scope("sum_quarters"):
        passed_top, passed_bottom = forward(far_top, 1), back(far_bottom, 1)
        from_left_bottom, from_right_top = forward(right_bottom, 1), back(left_top, 1)
        from_left_top = forward((right_top + passed_top.astype(F32)).astype(BF), 1)
        from_right_bottom = back((left_bottom + passed_bottom.astype(F32)).astype(BF), 1)
        summed = sum_halves(
            (own_top, from_left_top, from_right_top),
            (own_bottom, from_left_bottom, from_right_bottom),
        )
    with jax.named_scope("return_tokens"):
        returned = to_experts(summed.reshape(experts, capacity // 2, 2, quarter))
        rows = returned.reshape(slots, quarter)
        group_rows = lax.dot_general(
            select, rows, (((0,), (0,)), ((), ())), preferred_element_type=F32
        ).astype(BF)
        parts = [group_rows[k * own_rows : (k + 1) * own_rows] for k in range(4)]
        blocks = [parts[0]] + [forward(parts[k], ahead[k]) for k in (1, 2, 3)]
        return join_columns(blocks, x, [-r for r in ahead])


def solution(mesh):
    placed = (
        P(("expert", "etp"), None),
        P(("expert", "etp"), None),
        P(("expert", "etp"), None),
        P(("expert", "etp")),
        P("expert", None, "etp"),
        P("expert", None, "etp"),
    )
    return jax.shard_map(
        on_device, mesh=mesh, in_specs=placed, out_specs=P(("expert", "etp"), None), check_vma=False
    )
```

```python
import jax
import jax.numpy as jnp
from jax import lax
from jax.experimental import pallas as pl
from jax.experimental.pallas import tpu as pltpu
from jax.sharding import PartitionSpec as P

BF = jnp.bfloat16
F32 = jnp.float32


def cost(flops, nbytes, trans=0):
    return pl.CostEstimate(flops=flops, bytes_accessed=nbytes, transcendentals=trans)


def params(megabytes=20):
    return pltpu.CompilerParams(
        dimension_semantics=("arbitrary",), vmem_limit_bytes=megabytes * 1024 * 1024
    )


def in_hbm(array):
    return pltpu.with_memory_space_constraint(array, pltpu.HBM)


def quarter_at(x_ref, ahead):
    return (x_ref[0] + ahead) & 3


def split_columns(array, x, offsets, scale=None):
    rows, columns = array.shape
    width = columns // 4

    def kernel(x_ref, *refs):
        scale_refs = refs[4:-4]
        for source, target in zip(refs[:4], refs[-4:]):
            if scale_refs:
                target[...] = (source[...].astype(F32) * scale_refs[0][...]).astype(BF)
            else:
                target[...] = source[...]

    def block(offset):
        return pl.BlockSpec((rows, width), lambda i, x_ref: (0, quarter_at(x_ref, offset)))

    extra = [] if scale is None else [scale]
    return pl.pallas_call(
        kernel,
        grid_spec=pltpu.PrefetchScalarGridSpec(
            num_scalar_prefetch=1,
            grid=(1,),
            in_specs=[block(offset) for offset in offsets]
            + [pl.BlockSpec((rows, 1), lambda i, x_ref: (0, 0)) for _ in extra],
            out_specs=[pl.BlockSpec((rows, width), lambda i, x_ref: (0, 0))] * 4,
        ),
        out_shape=[jax.ShapeDtypeStruct((rows, width), BF)] * 4,
        compiler_params=params(),
        cost_estimate=cost(rows * columns, 4 * rows * columns),
        name="split_columns",
    )(x, array, array, array, array, *extra)


def join_columns(blocks, x, offsets):
    rows, width = blocks[0].shape

    def kernel(x_ref, b0, b1, b2, b3, out):
        for offset, block in zip(offsets, (b0, b1, b2, b3)):
            start = pl.multiple_of(quarter_at(x_ref, offset) * width, 128)
            out[:, pl.ds(start, width)] = block[...]

    return pl.pallas_call(
        kernel,
        grid_spec=pltpu.PrefetchScalarGridSpec(
            num_scalar_prefetch=1,
            grid=(1,),
            in_specs=[pl.BlockSpec((rows, width), lambda i, x_ref: (0, 0))] * 4,
            out_specs=pl.BlockSpec((rows, 4 * width), lambda i, x_ref: (0, 0)),
        ),
        out_shape=jax.ShapeDtypeStruct((rows, 4 * width), BF),
        compiler_params=params(),
        cost_estimate=cost(0, 16 * rows * width),
        name="join_columns",
    )(x, *blocks)


def slot_index(group_routes, x, offsets, experts, capacity):
    own_rows = group_routes.shape[1]
    group = own_rows * len(offsets)

    def kernel(x_ref, all_routes, out):
        routes = jnp.concatenate(
            [all_routes[pl.ds(quarter_at(x_ref, offset), 1), :] for offset in offsets], axis=1
        )

        def places(axis):
            row = lax.broadcasted_iota(jnp.int32, (group, group), axis)
            block = row // own_rows
            offset = jnp.zeros_like(row)
            for k, value in enumerate(offsets):
                offset = jnp.where(block == k, value, offset)
            return ((x_ref[0] + offset) & 3) * own_rows + row % own_rows

        before = jnp.where(places(0) < places(1), 1.0, 0.0).astype(BF)
        same = lax.broadcasted_iota(jnp.int32, (experts, group), 0) == routes
        named = jnp.where(same, 1.0, 0.0)
        counts = jnp.dot(named.astype(BF), before, preferred_element_type=F32)
        rank = jnp.sum(named * counts, axis=0, keepdims=True).astype(jnp.int32)
        out[...] = routes * capacity + rank

    return pl.pallas_call(
        kernel,
        grid_spec=pltpu.PrefetchScalarGridSpec(
            num_scalar_prefetch=1,
            grid=(1,),
            in_specs=[pl.BlockSpec(group_routes.shape, lambda i, x_ref: (0, 0))],
            out_specs=pl.BlockSpec((1, group), lambda i, x_ref: (0, 0)),
        ),
        out_shape=jax.ShapeDtypeStruct((1, group), jnp.int32),
        compiler_params=params(),
        cost_estimate=cost(0, 0),
        name="slot_index",
    )(x, group_routes)


HIDDEN_TILE = 512
SCHEDULE_WEIGHT = 6


def up_sums(blocks, offsets, gate_weight, up_weight, x, so_far=()):
    rows, depth = blocks[0].shape
    hidden = gate_weight.shape[1]
    count = len(offsets)

    def kernel(x_ref, *refs):
        starts = refs[3 * count : -2]
        for n, out in enumerate(refs[-2:]):
            weights = refs[(1 + n) * count : (2 + n) * count]
            total = jnp.dot(refs[0][...], weights[0][...], preferred_element_type=F32)
            for block, w in zip(refs[1:count], weights[1:]):
                total += jnp.dot(block[...], w[...], preferred_element_type=F32)
            if starts:
                total += starts[n][...]
            out[...] = total

    def weight(offset):
        return pl.BlockSpec((depth, HIDDEN_TILE), lambda j, x_ref: (quarter_at(x_ref, offset), j))

    tiled = pl.BlockSpec((rows, HIDDEN_TILE), lambda j, x_ref: (0, j))
    if so_far:
        out_shape = [pltpu.HBM((rows, hidden), F32)] * 2
    else:
        out_shape = [jax.ShapeDtypeStruct((rows, hidden), F32)] * 2
    return pl.pallas_call(
        kernel,
        grid_spec=pltpu.PrefetchScalarGridSpec(
            num_scalar_prefetch=1,
            grid=(hidden // HIDDEN_TILE,),
            in_specs=[pl.BlockSpec((rows, depth), lambda j, x_ref: (0, 0))] * count
            + [weight(offset) for offset in offsets] * 2
            + [tiled] * len(so_far),
            out_specs=[tiled, tiled],
        ),
        out_shape=out_shape,
        compiler_params=params(),
        cost_estimate=cost(
            SCHEDULE_WEIGHT * 4 * count * rows * depth * hidden, 4 * count * depth * hidden + 16 * rows * hidden
        ),
        name="up_sums",
    )(x, *blocks, *([gate_weight] * count), *([up_weight] * count), *so_far)


CONTRACT_LAST = (((1,), (1,)), ((), ()))


def down_dot(gg, gu, wg, wu):
    total = lax.dot_general(gg, wg, CONTRACT_LAST, preferred_element_type=F32)
    return total + lax.dot_general(gu, wu, CONTRACT_LAST, preferred_element_type=F32)


def up_last(upper, lower, gate, up, offset, gate_weight, up_weight, x):
    half, depth = upper.shape
    rows, hidden = gate.shape

    def kernel(x_ref, top, bottom, g_in, u_in, wg, wu, for_gate, for_up):
        for k, t in enumerate((top, bottom)):
            part = slice(k * half, (k + 1) * half)
            g = g_in[part, :] + jnp.dot(t[...], wg[...], preferred_element_type=F32)
            u = u_in[part, :] + jnp.dot(t[...], wu[...], preferred_element_type=F32)
            s = 1.0 / (1.0 + jnp.exp(-g))
            for_gate[part, :] = (u * s * (1.0 + g * (1.0 - s))).astype(BF)
            for_up[part, :] = (g * s).astype(BF)

    weight = pl.BlockSpec((depth, HIDDEN_TILE), lambda j, x_ref: (quarter_at(x_ref, offset), j))
    tiled = pl.BlockSpec((rows, HIDDEN_TILE), lambda j, x_ref: (0, j))
    halves = [pl.BlockSpec((half, depth), lambda j, x_ref: (0, 0))] * 2
    return pl.pallas_call(
        kernel,
        grid_spec=pltpu.PrefetchScalarGridSpec(
            num_scalar_prefetch=1,
            grid=(hidden // HIDDEN_TILE,),
            in_specs=halves + [tiled] * 2 + [weight] * 2,
            out_specs=[tiled] * 2,
        ),
        out_shape=[pltpu.HBM((rows, hidden), BF)] * 2,
        compiler_params=params(),
        cost_estimate=cost(
            4 * rows * depth * hidden, 4 * depth * hidden + 12 * rows * hidden, rows * hidden
        ),
        name="up_last",
    )(x, upper, lower, gate, up, gate_weight, up_weight)


def down_first(scaled, for_gate, for_up, offset, gate_weight, up_weight, x):
    rows, hidden = scaled.shape
    depth = gate_weight.shape[0] // 4
    half = rows // 2

    def kernel(x_ref, h, a, b, wg, wu, gg_out, gu_out, out_top, out_bottom):
        for k, out in enumerate((out_top, out_bottom)):
            part = slice(k * half, (k + 1) * half)
            h_part = h[part, :].astype(F32)
            gg = (h_part * a[part, :].astype(F32)).astype(BF)
            gu = (h_part * b[part, :].astype(F32)).astype(BF)
            gg_out[part, :] = gg
            gu_out[part, :] = gu
            out[...] = down_dot(gg, gu, wg[...], wu[...]).astype(BF)

    weight = pl.BlockSpec((depth, hidden), lambda k, x_ref: (quarter_at(x_ref, offset), 0))
    whole = pl.BlockSpec((rows, hidden), lambda k, x_ref: (0, 0))
    halves = [pl.BlockSpec((half, depth), lambda k, x_ref: (0, 0))] * 2
    return pl.pallas_call(
        kernel,
        grid_spec=pltpu.PrefetchScalarGridSpec(
            num_scalar_prefetch=1,
            grid=(1,),
            in_specs=[whole] * 3 + [weight] * 2,
            out_specs=[whole] * 2 + halves,
        ),
        out_shape=[jax.ShapeDtypeStruct((rows, hidden), BF)] * 2
        + [jax.ShapeDtypeStruct((half, depth), BF)] * 2,
        compiler_params=params(megabytes=30),
        cost_estimate=cost(4 * rows * depth * hidden, 4 * depth * hidden + 10 * rows * hidden),
        name="down_first",
    )(x, scaled, in_hbm(for_gate), in_hbm(for_up), gate_weight, up_weight)


def down_halves(grad_gate, grad_up, gate_weight, up_weight, x, pieces, dtype):
    rows, hidden = grad_gate.shape
    depth = gate_weight.shape[0] // 4
    half = rows // 2
    count = len(pieces)

    def at_step(j, values):
        chosen = values[0]
        for k in range(1, count):
            chosen = jnp.where(j == k, values[k], chosen)
        return chosen

    def kernel(x_ref, gg, gu, wg, wu, *outs):
        for k in range(count):

            @pl.when(pl.program_id(0) == k)
            def _():
                outs[k][...] = down_dot(gg[...], gu[...], wg[...], wu[...]).astype(dtype)

    weight = pl.BlockSpec(
        (depth, hidden),
        lambda j, x_ref: (quarter_at(x_ref, at_step(j, [offset for offset, _ in pieces])), 0),
    )
    grads = pl.BlockSpec((half, hidden), lambda j, x_ref: (at_step(j, [k for _, k in pieces]), 0))
    return pl.pallas_call(
        kernel,
        grid_spec=pltpu.PrefetchScalarGridSpec(
            num_scalar_prefetch=1,
            grid=(count,),
            in_specs=[grads] * 2 + [weight] * 2,
            out_specs=[pl.BlockSpec((half, depth), lambda j, x_ref: (0, 0))] * count,
        ),
        out_shape=[jax.ShapeDtypeStruct((half, depth), dtype)] * count,
        compiler_params=params(),
        cost_estimate=cost(
            1 * count * half * depth * hidden, 4 * count * depth * hidden + 4 * count * half * hidden
        ),
        name="down_halves",
    )(x, grad_gate, grad_up, gate_weight, up_weight)


def sum_halves(upper, lower):
    rows, width = upper[0].shape
    count = len(upper)

    def kernel(*refs):
        out = refs[-1]
        for k, half in enumerate((refs[:count], refs[count : 2 * count])):
            total = half[0][...].astype(F32)
            for ref in half[1:]:
                total = total + ref[...].astype(F32)
            out[k * rows : (k + 1) * rows, :] = total.astype(BF)

    return pl.pallas_call(
        kernel,
        out_shape=jax.ShapeDtypeStruct((2 * rows, width), BF),
        compiler_params=pltpu.CompilerParams(vmem_limit_bytes=20 * 1024 * 1024),
        cost_estimate=cost(4 * rows * width, 16 * rows * width),
        name="sum_halves",
    )(*upper, *lower)


def on_device(tokens, hidden_grad, routes, exponents, gate_weight, up_weight):
    etp = lax.axis_size("etp")
    experts = lax.axis_size("expert")
    own_rows, features = tokens.shape
    capacity = 5 * own_rows * etp // (4 * experts)
    slots = experts * capacity
    quarter, hidden = features // 4, hidden_grad.shape[1] // 4
    x = lax.axis_index("etp").astype(jnp.int32).reshape(1)
    gate_w, up_w = in_hbm(gate_weight[0]), in_hbm(up_weight[0])
    tokens, hidden_grad = in_hbm(tokens), in_hbm(hidden_grad)

    def back(array, r):
        return lax.ppermute(array, "etp", [(i, (i - r) % etp) for i in range(etp)])

    def forward(array, r):
        return lax.ppermute(array, "etp", [(i, (i + r) % etp) for i in range(etp)])

    ahead = (0, 2, 1, 3)
    with jax.named_scope("group_exchange"):
        token_parts = split_columns(tokens, x, [-r for r in ahead])
        group_tokens = jnp.concatenate(
            [token_parts[0]] + [back(token_parts[k], ahead[k]) for k in (1, 2, 3)]
        )
        group_routes = lax.all_gather(routes.reshape(1, own_rows), "etp", axis=0, tiled=True)
        scales = jnp.exp2(exponents.astype(F32))[:, None]
        hidden_parts = split_columns(hidden_grad, x, [-r for r in ahead], scales)
        group_hidden = jnp.concatenate(
            [hidden_parts[0]] + [back(hidden_parts[k], ahead[k]) for k in (1, 2, 3)]
        )

    with jax.named_scope("slots"):
        slot = slot_index(group_routes, x, ahead, experts, capacity)
        select = (jnp.arange(slots, dtype=jnp.int32)[:, None] == slot).astype(BF)

    def pick(rows):
        return jnp.dot(select, rows, preferred_element_type=F32).astype(BF)

    def to_experts(array):
        return lax.all_to_all(array, "expert", split_axis=0, concat_axis=0, tiled=True)

    with jax.named_scope("send_tokens"):
        packed_tokens = pick(group_tokens).reshape(experts, capacity // 2, 2, quarter)
        packed_hidden = pick(group_hidden).reshape(experts, capacity * hidden // 128, 128)
        arrived, packed_hidden = lax.optimization_barrier((to_experts(packed_tokens), packed_hidden))
        own_block = arrived.reshape(slots, quarter)
    with jax.named_scope("send_hidden"):
        scaled = to_experts(packed_hidden).reshape(slots, hidden)

    half = slots // 2
    with jax.named_scope("gather_width"):
        own_sums = up_sums((own_block,), (0,), gate_w, up_w, x)
        left_block, right_block, *own_sums = lax.optimization_barrier(
            (forward(own_block, 1), back(own_block, 1), *own_sums)
        )
        far_upper, far_lower = forward(left_block[:half], 1), back(right_block[half:], 1)
    with jax.named_scope("pre_activations"):
        gate, up = up_sums((in_hbm(right_block), in_hbm(left_block)), (1, 3), gate_w, up_w, x, own_sums)
        for_gate, for_up = up_last(far_upper, far_lower, in_hbm(gate), in_hbm(up), 2, gate_w, up_w, x)
    with jax.named_scope("input_partials"):
        grad_gate, grad_up, far_top, far_bottom = down_first(
            scaled, for_gate, for_up, 2, gate_w, up_w, x
        )
        right_bottom, left_top = down_halves(
            grad_gate, grad_up, gate_w, up_w, x, ((1, 1), (3, 0)), BF
        )
        right_top, left_bottom = down_halves(
            grad_gate, grad_up, gate_w, up_w, x, ((1, 0), (3, 1)), F32
        )
        own_top, own_bottom = down_halves(
            grad_gate, grad_up, gate_w, up_w, x, ((0, 0), (0, 1)), F32
        )
    with jax.named_scope("sum_quarters"):
        passed_top, passed_bottom = forward(far_top, 1), back(far_bottom, 1)
        from_left_bottom, from_right_top = forward(right_bottom, 1), back(left_top, 1)
        from_left_top = forward((right_top + passed_top.astype(F32)).astype(BF), 1)
        from_right_bottom = back((left_bottom + passed_bottom.astype(F32)).astype(BF), 1)
        summed = sum_halves(
            (own_top, from_left_top, from_right_top),
            (own_bottom, from_left_bottom, from_right_bottom),
        )
    with jax.named_scope("return_tokens"):
        returned = to_experts(summed.reshape(experts, capacity // 2, 2, quarter))
        rows = returned.reshape(slots, quarter)
        group_rows = lax.dot_general(
            select, rows, (((0,), (0,)), ((), ())), preferred_element_type=F32
        ).astype(BF)
        parts = [group_rows[k * own_rows : (k + 1) * own_rows] for k in range(4)]
        order = (0, 2, 3, 1)
        blocks = [forward(parts[k], ahead[k]) if k else parts[0] for k in order]
        return join_columns(blocks, x, [-ahead[k] for k in order])


def solution(mesh):
    placed = (
        P(("expert", "etp"), None),
        P(("expert", "etp"), None),
        P(("expert", "etp"), None),
        P(("expert", "etp")),
        P("expert", None, "etp"),
        P("expert", None, "etp"),
    )
    return jax.shard_map(
        on_device, mesh=mesh, in_specs=placed, out_specs=P(("expert", "etp"), None), check_vma=False
    )
```
